32 devices in a mesh: grid: 8 (over z, y), tile: 4 (over x, core).
Axes of the slice: x: 2, y: 2, z: 4, core: 2. Of those that a mesh axis runs over, the one named last changes fastest.
Arguments:
- point_values: bfloat16 [256, 16384], P('grid', 'tile'), may hold values from -1.75 to 1.75
- sig_blocks: int32 [8, 16], P('grid'), may hold values from 0 to 31, as said below
- density: bfloat16 [16384, 16384], P('grid', 'tile'), may hold values from -0.0625 to 0.0625
- coulomb_core: bfloat16 [512, 512], replicated, may hold values from -0.25 to 0.25
- screen_mask: int32 [32, 32], replicated, may hold values 0 or 1
- ao_centers: float32 [3, 16384], replicated, may hold values from -1 to 1
- ao_widths: float32 [16384], replicated, may hold values from 0.25 to 1
- point_coords: float32 [3, 256], P(None, 'grid'), may hold values from -1 to 1
- lmo_coeffs: bfloat16 [16384, 1024], P('tile'), may hold values from -0.0625 to 0.0625
- domain_blocks: int32 [4, 16], replicated, may hold values from 0 to 31, as said below
Outputs:
- half: bfloat16 [1024, 16384], P('tile', 'grid')
The draws below stay inside these ranges and needn't reach their ends.
Inputs may be any that keep to these rules, and one draw needn't show every extreme that they name: `sig_blocks`: each batch names 16 different AO blocks. `domain_blocks`: each strip's 16 blocks are different, and every AO block lies in the domain of some strip.
All inputs are finite; a program needn't handle non-finite values.
Results may differ from the reference program's by a relative error of at most 0.02.
Values may be sent and summed in bfloat16 or wider, within the bound.
A program may use at most 128 MiB of HBM per device.

```python
import math
import jax
import jax.numpy as jnp
from jax import lax

NAO = 16384
BLK = 512
BP = 32
LSTRIP = 256
DOMN = 16
BASIS_GROUP_NUM = 32
SIGN = 16
NBATCH = 8
POINTS = 256
CT = 4096
NSTRIP = 4
NLMO = 1024
N_TILE = 4


def draw_sig_blocks(key, part):
    preferred_sequence = jax.random.permutation(jax.random.fold_in(key, 7), BASIS_GROUP_NUM)
    preference_increment = jnp.where(preferred_sequence < 4, 512, 0)
    raw_ranking_weights = jax.random.randint(jax.random.fold_in(key, 8), (NBATCH, BASIS_GROUP_NUM), 0, 1024)
    group_ranking_weights = (raw_ranking_weights + preference_increment[None, :]) * BASIS_GROUP_NUM + jnp.arange(BASIS_GROUP_NUM, dtype=jnp.int32)[None, :]
    return lax.top_k(group_ranking_weights, SIGN)[1].astype(jnp.int32)


def draw_domain_blocks(key, part):
    shuffled = jax.random.permutation(jax.random.fold_in(key, 9), BASIS_GROUP_NUM)
    window_starts = jnp.arange(NSTRIP, dtype=jnp.int32) * (BASIS_GROUP_NUM // NSTRIP)
    positions = (window_starts[:, None] + jnp.arange(DOMN, dtype=jnp.int32)[None, :]) % BASIS_GROUP_NUM
    return shuffled[positions].astype(jnp.int32)


def set_ends(drawn, own_key, low, largest):
    shape = drawn.shape
    place = [jax.random.randint(jax.random.fold_in(own_key, axis), (), 0, shape[axis]) for axis in range(len(shape))]
    drawn = drawn.at[tuple(place)].set(low)
    longest = shape.index(max(shape))
    place[longest] = (place[longest] + 1) % shape[longest]
    return drawn.at[tuple(place)].set(largest)


def block_scale(stream_key, extent, shards, low, high):
    factor_of = 1.0
    for position, parts in shards:
        draws = jax.random.uniform(jax.random.fold_in(jax.random.fold_in(stream_key, 6), position), (parts,), jnp.float32, low / len(shards), high / len(shards))
        factor_of = factor_of * jnp.repeat(jnp.exp(draws), extent[position] // parts).reshape((-1,) + (1,) * (len(extent) - 1 - position))
    return factor_of


def scatter_about(key, dims, width, bound, cuts=(), kind=jnp.bfloat16):
    result = width * jax.random.normal(key, dims, jnp.float32)
    if cuts:
        result = result * block_scale(key, dims, cuts, -0.22, 0.18)
    return jnp.clip(result, -bound, bound).astype(kind)


def setup_inputs(seed: int = 0) -> dict:
    seeds = jax.random.split(jax.random.key(seed), 11)
    return {
        "point_values": scatter_about(seeds[0], (POINTS, NAO), 0.3, 1.75, ((0, 8), (1, 4))),
        "sig_blocks": draw_sig_blocks(jax.random.fold_in(seeds[10], 71), 0),
        "density": scatter_about(seeds[2], (NAO, NAO), (SIGN * BLK) ** -0.5, 0.0625, ((0, 8), (1, 4))),
        "coulomb_core": scatter_about(seeds[3], (BLK, BLK), BLK ** -0.5, 0.25),
        "screen_mask": set_ends((jax.random.randint(seeds[4], (BASIS_GROUP_NUM, BASIS_GROUP_NUM), 0, 4) < 3).astype(jnp.int32), jax.random.fold_in(seeds[4], 1), 0, 1),
        "ao_centers": jnp.clip(jax.random.uniform(seeds[5], (3, NAO), jnp.float32, -1.0, 1.0), -1.0, 1.0),
        "ao_widths": jnp.clip(jnp.exp(jax.random.uniform(seeds[6], (NAO,), jnp.float32, math.log(0.25), math.log(1.0))), 0.25, 1.0),
        "point_coords": jnp.clip(jax.random.uniform(seeds[7], (3, POINTS), jnp.float32, -1.0, 1.0) * block_scale(seeds[7], (3, POINTS), ((1, 8),), -0.4, 0.0), -1.0, 1.0),
        "lmo_coeffs": scatter_about(seeds[8], (NAO, NLMO), (DOMN * BLK) ** -0.5, 0.0625, ((0, 4),)),
        "domain_blocks": draw_domain_blocks(jax.random.fold_in(seeds[10], 71), 0),
    }


highest = lax.Precision.HIGHEST

def batch_factors(values, block_list, coords, density_blocks, coulomb_core, screen_mask, ao_centers, ao_widths):
    sig_density = density_blocks[block_list][:, :, block_list, :].astype(jnp.float32)
    sig_values = values.reshape(BP, BASIS_GROUP_NUM, BLK)[:, block_list, :]
    per_column = jnp.einsum('kajc,pjc->jpka', sig_density, sig_values.astype(jnp.float32), precision=highest)
    owners = block_list // (CT // BLK)
    owner_onehot = (owners[:, None] == jnp.arange(N_TILE, dtype=jnp.int32)[None, :]).astype(jnp.float32)
    by_tile = jnp.einsum('jt,jpka->tpka', owner_onehot, per_column, precision=highest)
    rounded = lax.optimization_barrier(by_tile.astype(jnp.bfloat16)).astype(jnp.float32)
    density_term = lax.optimization_barrier(jnp.sum(rounded, axis=0))
    offsets = ao_centers[:, None, :] - coords[:, :, None]
    coefficient = 1.0 / jnp.sqrt(lax.optimization_barrier(jnp.sum(offsets * offsets, axis=0)) + ao_widths[None, :])
    sig_coeff = coefficient.reshape(BP, BASIS_GROUP_NUM, BLK)[:, block_list, :]
    weighted = sig_coeff * density_term
    screen = screen_mask[block_list][:, block_list].astype(jnp.float32)
    screened = jnp.einsum('kj,pja->pka', screen, weighted, precision=highest)
    mixed_term = jnp.einsum('ab,pkb->pka', coulomb_core.astype(jnp.float32), screened, precision=highest)
    potential = (sig_coeff * mixed_term).astype(jnp.bfloat16)
    return (sig_values, potential)

def reference(point_values, sig_blocks, density, coulomb_core, screen_mask, ao_centers, ao_widths, point_coords, lmo_coeffs, domain_blocks):
    density_blocks = density.reshape(BASIS_GROUP_NUM, BLK, BASIS_GROUP_NUM, BLK)
    values = point_values.reshape(NBATCH, BP, NAO)
    coords = jnp.transpose(point_coords.reshape(3, NBATCH, BP), (1, 0, 2))

    def one_batch(entries):
        return batch_factors(entries[0], entries[1], entries[2], density_blocks, coulomb_core, screen_mask, ao_centers, ao_widths)
    sig_values, potentials = lax.map(one_batch, (values, sig_blocks, coords))

    def accumulate(running_sum, entries):
        batch_values, batch_pots, block_list = entries
        tile_sum = jnp.einsum('pka,pjc->kjac', batch_values.astype(jnp.float32), batch_pots.astype(jnp.float32), precision=highest)
        return (running_sum.at[block_list[:, None], :, block_list[None, :], :].add(tile_sum), None)
    running_sum = jnp.zeros((BASIS_GROUP_NUM, BLK, BASIS_GROUP_NUM, BLK), jnp.float32)
    running_sum, unused = lax.scan(accumulate, running_sum, (sig_values, potentials, sig_blocks))
    exch_tile = running_sum.astype(jnp.bfloat16)
    strip_coeffs = jnp.transpose(lmo_coeffs.reshape(BASIS_GROUP_NUM, BLK, NSTRIP, LSTRIP), (2, 0, 1, 3))

    def one_strip(entries):
        coeff_strip, domain = entries
        exch_columns = exch_tile[:, :, domain, :].reshape(NAO, DOMN * BLK)
        coeff_rows = coeff_strip[domain].reshape(DOMN * BLK, LSTRIP)
        return lax.dot_general(coeff_rows, exch_columns, (((0,), (1,)), ((), ())), preferred_element_type=jnp.float32).astype(jnp.bfloat16)
    halves = lax.map(one_strip, (strip_coeffs, domain_blocks))
    return halves.reshape(NLMO, NAO)
```

```python
import functools
import math

import jax
import jax.numpy as jnp
from jax import lax
from jax.experimental import pallas as pl
from jax.experimental.pallas import tpu as pltpu
from jax.sharding import PartitionSpec as P

MESH = pl.DeviceIdType.MESH
VMEM_LIMIT = 60 * 1024 * 1024
CHUNK = 512
EARLY = 1
LAG = 3
f32 = jnp.float32
bf16 = jnp.bfloat16
NT = (((1,), (1,)), ((), ()))
TN = (((0,), (0,)), ((), ()))


def grid_split(grid_count):
    inner = max(1, math.isqrt(max(1, grid_count // 2)))
    while grid_count % inner:
        inner -= 1
    return grid_count // inner, inner


def remote(src, dst, send_sem, recv_sem, device):
    return pltpu.make_async_remote_copy(
        src_ref=src,
        dst_ref=dst,
        send_sem=send_sem,
        recv_sem=recv_sem,
        device_id=device,
        device_id_type=MESH,
    )


def listed(table_ref, row, block_id):
    flag = jnp.float32(0.0)
    for i in range(table_ref.shape[1]):
        flag = jnp.where(table_ref[row, i] == block_id, jnp.float32(1.0), flag)
    return flag


def dot(a, b, dims=(((1,), (0,)), ((), ()))):
    return lax.dot_general(a, b, dims, preferred_element_type=f32)


def kernel(
    nz,
    ny,
    nx,
    sig_ref,
    domain_ref,
    value_ref,
    density_hbm,
    core_hbm,
    mask_hbm,
    centers_hbm,
    widths_hbm,
    coords_hbm,
    lmo_hbm,
    out_ref,
    all_ref,
    density_ref,
    acc_ref,
    part_ref,
    sibling_ref,
    pair_ref,
    peer_ref,
    total_ref,
    back_ref,
    core_ref,
    mask_ref,
    centers_ref,
    widths_ref,
    coords_ref,
    lmo_ref,
    scaled_ref,
    spread_ref,
    weighted_ref,
    pot_ref,
    got_ref,
    flat_ref,
    send_ref,
    share_ref,
    own_ref,
    weights_ref,
    rows_ref,
    flags_ref,
    zs,
    zr,
    ds_,
    dr,
    ys,
    yr,
    es,
    er,
    local_sem,
    load_sem,
    cs,
    cr,
    xs,
    xr,
    gs,
    gr,
    vs,
    vr,
    ws,
    wr,
    fs,
    fr,
):
    grid_count, tile_count, nc = nz * ny, nx * 2, 2
    batch, cols = value_ref.shape
    rows = density_ref.shape[0]
    block = core_ref.shape[0]
    blocks = mask_ref.shape[0]
    slab = batch // tile_count
    tile_blocks = cols // block
    row_blocks = rows // block
    chunks = cols // CHUNK
    strips = domain_ref.shape[0]
    strip_width = lmo_ref.shape[1] // strips
    per_tile = strips // tile_count

    g, t = lax.axis_index("grid"), lax.axis_index("tile")
    z, y = g // ny, g % ny
    x, c = t // nc, t % nc
    place = c * nx + x
    has_left, has_right = z > 0, z < nz - 1
    left = (lax.rem(z + nz - 1, nz) * ny + y, t)
    right = (lax.rem(z + 1, nz) * ny + y, t)
    y_peers = [(z * ny + lax.rem(y + d, ny), t) for d in range(1, ny)]
    x_peers = [(g, lax.rem(x + d, nx) * nc + c) for d in range(1, nx)]
    sibling = (g, x * nc + (1 - c))
    far_tiles = [
        lax.rem(x + d, nx) * nc + (c if e == 0 else 1 - c) for d in range(1, nx) for e in range(nc)
    ]
    tile_order = far_tiles + [x * nc + (1 - c), t]

    loads = [
        pltpu.make_async_copy(src, dst, load_sem.at[i])
        for i, (src, dst) in enumerate(
            [
                (coords_hbm, coords_ref),
                (widths_hbm, widths_ref),
                (centers_hbm, centers_ref),
                (mask_hbm, mask_ref),
                (core_hbm, core_ref),
                (density_hbm, density_ref),
                (lmo_hbm, lmo_ref),
            ]
        )
    ]
    small_loads, core_load, density_load, lmo_load = loads[:4], loads[4], loads[5], loads[6]

    barrier = pltpu.get_barrier_semaphore()

    def hello(device):
        pl.semaphore_signal(barrier, inc=1, device_id=device, device_id_type=MESH)

    @pl.when(has_left)
    def _():
        hello(left)

    @pl.when(has_right)
    def _():
        hello(right)

    for peer in y_peers + [(g, tile) for tile in tile_order[:-1]]:
        hello(peer)

    for m in range(tile_blocks):
        lanes = slice(m * block, (m + 1) * block)
        flag = listed(sig_ref, 0, t * tile_blocks + m)
        all_ref[g, :, lanes] = (value_ref[:, lanes].astype(f32) * flag).astype(bf16)

    neighbours = (
        ny - 1 + tile_count - 1 + jnp.where(has_left, 1, 0) + jnp.where(has_right, 1, 0)
    )
    pl.semaphore_wait(barrier, neighbours)

    def source(line, d):
        return line * ny + lax.rem(y + ny - d, ny)

    def piece(src, q):
        return all_ref.at[src, :, pl.ds(q * CHUNK, CHUNK)]

    def z_sems(lane, line, d, q):
        if d == 0:
            return zs.at[lane, line], zr.at[lane, line, q]
        return ds_.at[lane, line, d - 1], dr.at[lane, line, d - 1, q]

    def along(line, d, q, lane):
        spot = piece(source(line, d), q)
        send, recv = z_sems(lane, line, d, q)
        return remote(spot, spot, send, recv, left if lane else right)

    def across(line, d, q):
        spot = piece(source(line, 0), q)
        return remote(spot, spot, ys.at[d - 1, line], yr.at[d - 1, line, q], y_peers[d - 1])

    def along_arrived(line, d, q, lane):
        spot = piece(source(line, d), q)
        send, recv = z_sems(lane, line, d, q)
        remote(spot, spot, send, recv, right).wait_recv()

    def across_arrived(line, d, q):
        spot = piece(source(line, d), q)
        remote(spot, spot, ys.at[d - 1, line], yr.at[d - 1, line, q], right).wait_recv()

    def both_ways(d, q):
        @pl.when(has_right)
        def _():
            along(z, d, q, 0).start()

        @pl.when(has_left)
        def _():
            along(z, d, q, 1).start()

    for q in range(chunks):
        for d in range(1, ny):
            across(z, d, q).start()
        both_ways(0, q)
    for load in loads:
        load.start()

    for load in small_loads:
        load.wait()
    point = lax.broadcasted_iota(jnp.int32, (slab, batch), 1)
    wanted = lax.broadcasted_iota(jnp.int32, (slab, batch), 0) + place * slab
    here = [
        jnp.sum(
            jnp.where(point == wanted, coords_ref[d : d + 1, :], 0.0), axis=1, keepdims=True
        )
        for d in range(3)
    ]
    for j in range(blocks):
        lanes = slice(j * block, (j + 1) * block)
        distance = None
        for d in range(3):
            offset = centers_ref[d : d + 1, lanes] - here[d]
            distance = offset * offset if distance is None else distance + offset * offset
        coefficient = 1.0 / jnp.sqrt(distance + widths_ref[0:1, lanes])
        scaled_ref[j * slab : (j + 1) * slab, :] = coefficient * listed(sig_ref, 0, j)

    for q in range(EARLY):
        for d in range(1, ny):
            across_arrived(z, d, q)
            both_ways(d, q)

    total_rows = blocks * slab
    row = lax.broadcasted_iota(jnp.int32, (total_rows, blocks), 0)
    first = lax.broadcasted_iota(jnp.int32, (total_rows, blocks), 1) * slab
    expand = jnp.where((row >= first) & (row < first + slab), 1.0, 0.0).astype(bf16)
    screen = mask_ref[...].astype(f32).astype(bf16)
    spread = dot(dot(expand, screen).astype(bf16), expand, NT)
    row = lax.broadcasted_iota(jnp.int32, (total_rows, total_rows), 0)
    column = lax.broadcasted_iota(jnp.int32, (total_rows, total_rows), 1)
    spread_ref[...] = jnp.where(
        lax.rem(row, slab) == lax.rem(column, slab), spread, 0.0
    ).astype(bf16)
    for s in range(strips):
        for m in range(tile_blocks):
            flags_ref[s, m] = listed(domain_ref, s, t * tile_blocks + m)

    near = jnp.minimum(z, nz - 1 - z)

    def nearest(i):
        paired = z - (i + 1) // 2 if i % 2 else z + i // 2
        single = jnp.where(z < nz - 1 - z, i, nz - 1 - i)
        return jnp.where(i <= 2 * near, paired, single)

    order = [nearest(i) for i in range(nz)]

    row_start = pl.multiple_of((g * rows) % cols, rows)
    owner = (g * rows) // cols
    is_owner = owner == t
    in_column = owner % nc == c

    def share(line, d):
        src = source(line, d)

        @pl.when(is_owner)
        def _():
            for i, peer in enumerate(x_peers + [sibling]):
                remote(
                    all_ref.at[src, :, pl.ds(row_start, rows)],
                    rows_ref.at[src],
                    es.at[i],
                    er.at[src],
                    peer,
                ).start()

    def take_across(i):
        for d in range(1, ny):
            for q in range(EARLY if i == 0 else EARLY, chunks):
                across_arrived(order[i], d, q)
            share(order[i], d)

    def serve(step, q):
        for lane, line, here_, onward in (
            (0, z - step, z >= step, has_right),
            (1, z + step, z + step <= nz - 1, has_left),
        ):

            @pl.when(here_)
            def _():
                for d in range(ny if q < EARLY else 1):
                    along_arrived(line, d, q, lane)

                    @pl.when(onward)
                    def _():
                        along(line, d, q, lane).start()

                if q >= EARLY:
                    for d in range(1, ny):
                        across(line, d, q).start()

    def gathered(q):
        return all_ref[:, :, q * CHUNK : (q + 1) * CHUNK].reshape(grid_count * batch, CHUNK)

    def product(q, i):
        return dot(
            gathered(q), density_ref[i * block : (i + 1) * block, q * CHUNK : (q + 1) * CHUNK], NT
        )

    late = max(1, nz - 2)

    def multiply(q):
        if q >= EARLY:
            for i in range(late, nz):
                for d in range(1, ny):
                    across_arrived(order[i], d, q)
        if q == chunks - 1:
            return
        for i in range(row_blocks):
            lanes = slice(i * block, (i + 1) * block)
            if q == 0:
                acc_ref[:, lanes] = product(q, i)
            else:
                acc_ref[:, lanes] = acc_ref[:, lanes] + product(q, i)

    share(z, 0)
    for step in range(1, nz):
        last = step == nz - 1
        if last:
            density_load.wait()
        for q in range(chunks):
            serve(step, q)
            if last and q >= LAG:
                multiply(q - LAG)
        if step < late + 1 and step - 1 < late:
            take_across(step - 1)
        if not last:
            share(order[step], 0)
    if nz == 1:
        density_load.wait()
    for q in range(max(0, chunks - LAG) if nz > 1 else 0, chunks):
        multiply(q)

    def core_copy(i):
        return remote(part_ref.at[i, 1 - c], sibling_ref.at[i], cs.at[i], cr.at[i], sibling)

    def pair_copy(i, d):
        return remote(
            pair_ref.at[i, d - 1], peer_ref.at[i, d - 1], xs.at[i, d - 1], xr.at[i, d - 1],
            x_peers[d - 1],
        )

    def finish_product(i):
        lanes = slice(i * block, (i + 1) * block)
        value = product(chunks - 1, i)
        if chunks > 1:
            value = value + acc_ref[:, lanes]
        if slab % 8 == 0:
            split = value.reshape(grid_count, nc, nx, slab, block).astype(bf16)
            for e in range(nc):
                part_ref[i, e] = split[:, e]
        else:
            for n in range(grid_count):
                for e in range(nc):
                    for h in range(nx):
                        start = ((n * nc + e) * nx + h) * slab
                        part_ref[i, e, n, h] = value[start : start + slab].astype(bf16)
        core_copy(i).start()

    def exchange(i):
        core_copy(i).wait_recv()
        for d in range(1, nx):
            column = lax.rem(x + d, nx)

            @pl.loop(0, grid_count)
            def _(n):
                pair_ref[i, d - 1, n] = (
                    part_ref[i, c, n, column].astype(f32)
                    + sibling_ref[i, n, column].astype(f32)
                ).astype(bf16)

            pair_copy(i, d).start()

    for i in range(row_blocks):
        finish_product(i)
        if i:
            exchange(i - 1)
    exchange(row_blocks - 1)

    for i in range(late, nz):
        if i == nz - 1 and nz > 1:
            share(order[i], 0)
        for d in range(1, ny):
            share(order[i], d)

    own_rows = pltpu.make_async_copy(
        all_ref.at[:, :, pl.ds(row_start, rows)], rows_ref, local_sem
    )

    @pl.when(is_owner)
    def _():
        own_rows.start()

    far_order = [
        (order[i], d) for i in range(nz - 1, -1, -1) for d in range(ny) if i or d
    ]
    targets = [(line * ny + lax.rem(y + d, ny), n) for n, (line, d) in enumerate(far_order)]
    senders = [line * ny + lax.rem(y + ny - d, ny) for line, d in far_order]

    def return_copy(i, target, n):
        return remote(
            total_ref.at[i, target], back_ref.at[g, i], gs.at[i, n], gr.at[i, g], (target, t)
        )

    for i in range(row_blocks):
        for d in range(1, nx):
            pair_copy(i, d).wait_recv()

        @pl.loop(0, grid_count)
        def _(n):
            value = part_ref[i, c, n, x].astype(f32) + sibling_ref[i, n, x].astype(f32)
            for d in range(1, nx):
                value = value + peer_ref[i, d - 1, n].astype(f32)
            total_ref[i, n] = value.astype(bf16)

        for target, n in targets:
            return_copy(i, target, n).start()
        back_ref[g, i] = total_ref[i, g]

    @pl.when(jnp.logical_and(in_column, jnp.logical_not(is_owner)))
    def _():
        for src in range(grid_count):
            spot = rows_ref.at[src]
            pass_on = remote(spot, spot, es.at[nx - 1], er.at[src], sibling)
            pass_on.wait_recv()
            pass_on.start()

    core_load.wait()
    for sender in reversed(senders):
        for i in range(row_blocks):
            spot = back_ref.at[sender, i]
            remote(spot, spot, gs.at[i, 0], gr.at[i, sender], right).wait_recv()
    for j in range(blocks):
        span = slice(j * slab, (j + 1) * slab)
        weighted_ref[span, :] = scaled_ref[span, :] * back_ref[
            j // row_blocks, j % row_blocks
        ].astype(f32)
    weighted = weighted_ref[...].astype(bf16)

    tile_rows = tile_blocks * slab
    v_copies = []
    for n, tile in enumerate(tile_order):
        span = pl.ds(pl.multiple_of(tile * tile_rows, tile_rows), tile_rows)
        screened = dot(spread_ref[span, :], weighted).astype(bf16)
        potential = scaled_ref[span, :] * dot(screened, core_ref[...], NT)
        is_own = n == len(tile_order) - 1
        for m in range(tile_blocks):
            value = potential[m * slab : (m + 1) * slab, :].astype(bf16)
            if is_own:
                got_ref[place, m] = value
            else:
                pot_ref[n, m] = value
        if not is_own:
            copy = remote(
                pot_ref.at[n], got_ref.at[place], vs.at[n], vr.at[place], (g, tile)
            )
            copy.start()
            v_copies.append(copy)

    lmo_load.wait()
    places = [(tile % nc) * nx + tile // nc for tile in tile_order]
    for n in reversed(range(tile_count - 1)):
        spot = got_ref.at[places[n]]
        remote(spot, spot, vs.at[n], vr.at[places[n]], right).wait_recv()
    for i in range(tile_count):
        for m in range(tile_blocks):
            flat_ref[i * slab : (i + 1) * slab, m * block : (m + 1) * block] = got_ref[
                i, m
            ].astype(f32)

    w_copies = []
    own_total = None
    for n, tile in enumerate(tile_order):
        pieces = []
        for k in range(per_tile):
            s = tile * per_tile + k
            kept = jnp.concatenate(
                [
                    (flat_ref[:, m * block : (m + 1) * block] * flags_ref[s, m]).astype(bf16)
                    for m in range(tile_blocks)
                ],
                axis=1,
            )
            start = pl.multiple_of(s * strip_width, strip_width)
            pieces.append(dot(kept, lmo_ref[:, pl.ds(start, strip_width)]))
        value = pieces[0] if per_tile == 1 else jnp.concatenate(pieces, axis=1)
        if n < tile_count - 1:
            send_ref[n] = value.astype(bf16)
            copy = remote(send_ref.at[n], share_ref.at[t], ws.at[n], wr.at[t], (g, tile))
            copy.start()
            w_copies.append(copy)
        else:
            own_total = value
    for n in reversed(range(tile_count - 1)):
        tile = tile_order[n]
        spot = share_ref.at[tile]
        remote(spot, spot, ws.at[n], wr.at[tile], right).wait_recv()
        own_total = own_total + share_ref[tile].astype(f32)
    own_ref[...] = own_total.astype(bf16)
    f_copies = []
    for target, n in targets:
        copy = remote(own_ref, weights_ref.at[g], fs.at[n], fr.at[g], (target, t))
        copy.start()
        f_copies.append(copy)
    weights_ref[g] = own_ref[...]

    @pl.when(is_owner)
    def _():
        own_rows.wait()

    @pl.when(jnp.logical_not(in_column))
    def _():
        for src in range(grid_count):
            spot = rows_ref.at[src]
            remote(spot, spot, es.at[0], er.at[src], right).wait_recv()

    for sender in reversed(senders):
        spot = weights_ref.at[sender]
        remote(spot, spot, fs.at[0], fr.at[sender], right).wait_recv()
    out_ref[...] = dot(
        weights_ref[...].reshape(grid_count * batch, weights_ref.shape[2]),
        rows_ref[...].reshape(grid_count * batch, rows),
        TN,
    ).astype(bf16)

    for line in range(nz):
        for lane, sent in (
            (0, jnp.logical_and(has_right, line <= z)),
            (1, jnp.logical_and(has_left, line >= z)),
        ):

            @pl.when(sent)
            def _():
                spot = all_ref.at[0]
                remote(spot, spot, zs.at[lane, line], zr.at[0, 0, 0], right).wait_send()
                spot = all_ref.at[0, :, pl.ds(0, EARLY * CHUNK)]
                for d in range(1, ny):
                    remote(
                        spot, spot, ds_.at[lane, line, d - 1], zr.at[0, 0, 0], right
                    ).wait_send()

    for i in range(nz):
        width = cols if i == 0 else cols - EARLY * CHUNK
        spot = all_ref.at[0, :, pl.ds(0, width)]
        for d in range(1, ny):
            remote(spot, spot, ys.at[d - 1, order[i]], zr.at[0, 0, 0], right).wait_send()

    @pl.when(is_owner)
    def _():
        for i in range(nx):
            remote(rows_ref, rows_ref, es.at[i], er.at[0], right).wait_send()

    @pl.when(jnp.logical_and(in_column, jnp.logical_not(is_owner)))
    def _():
        remote(rows_ref, rows_ref, es.at[nx - 1], er.at[0], right).wait_send()

    for i in range(row_blocks):
        core_copy(i).wait_send()
        for d in range(1, nx):
            pair_copy(i, d).wait_send()
        for target, n in targets:
            return_copy(i, target, n).wait_send()
    for copy in v_copies + w_copies + f_copies:
        copy.wait_send()


def shards(
    point_values,
    sig_blocks,
    density,
    coulomb_core,
    screen_mask,
    ao_centers,
    ao_widths,
    point_coords,
    lmo_coeffs,
    domain_blocks,
):
    grid_count, tile_count = lax.axis_size("grid"), lax.axis_size("tile")
    nz, ny = grid_split(grid_count)
    nc, nx = 2, tile_count // 2
    rows, cols = density.shape
    batch = point_values.shape[0]
    block = coulomb_core.shape[0]
    total = ao_widths.shape[0]
    blocks = total // block
    slab = batch // tile_count
    strip = lmo_coeffs.shape[1] // tile_count
    tile_blocks, row_blocks, chunks = cols // block, rows // block, cols // CHUNK
    dma = pltpu.SemaphoreType.DMA
    smem = pl.BlockSpec(memory_space=pltpu.SMEM)
    vmem = pl.BlockSpec(memory_space=pltpu.VMEM)
    anywhere = pl.BlockSpec(memory_space=pl.ANY)
    side = max(1, ny - 1)
    return pl.pallas_call(
        functools.partial(kernel, nz, ny, nx),
        out_shape=jax.ShapeDtypeStruct((strip, rows), bf16),
        in_specs=[smem, smem, vmem] + [anywhere] * 7,
        out_specs=vmem,
        scratch_shapes=[
            pltpu.VMEM((grid_count, batch, cols), bf16),
            pltpu.VMEM((rows, cols), bf16),
            pltpu.VMEM((grid_count * batch, rows), f32),
            pltpu.VMEM((row_blocks, nc, grid_count, nx, slab, block), bf16),
            pltpu.VMEM((row_blocks, grid_count, nx, slab, block), bf16),
            pltpu.VMEM((row_blocks, max(1, nx - 1), grid_count, slab, block), bf16),
            pltpu.VMEM((row_blocks, max(1, nx - 1), grid_count, slab, block), bf16),
            pltpu.VMEM((row_blocks, grid_count, slab, block), bf16),
            pltpu.VMEM((grid_count, row_blocks, slab, block), bf16),
            pltpu.VMEM(coulomb_core.shape, bf16),
            pltpu.VMEM(screen_mask.shape, jnp.int32),
            pltpu.VMEM(ao_centers.shape, f32),
            pltpu.VMEM((1, total), f32),
            pltpu.VMEM(point_coords.shape, f32),
            pltpu.VMEM(lmo_coeffs.shape, bf16),
            pltpu.VMEM((blocks * slab, block), f32),
            pltpu.VMEM((blocks * slab, blocks * slab), bf16),
            pltpu.VMEM((blocks * slab, block), f32),
            pltpu.VMEM((tile_count - 1, tile_blocks, slab, block), bf16),
            pltpu.VMEM((tile_count, tile_blocks, slab, block), bf16),
            pltpu.VMEM((batch, cols), f32),
            pltpu.VMEM((tile_count - 1, batch, strip), bf16),
            pltpu.VMEM((tile_count, batch, strip), bf16),
            pltpu.VMEM((batch, strip), bf16),
            pltpu.VMEM((grid_count, batch, strip), bf16),
            pltpu.VMEM((grid_count, batch, rows), bf16),
            pltpu.SMEM((domain_blocks.shape[0], tile_blocks), f32),
            dma((2, nz)),
            dma((2, nz, chunks)),
            dma((2, nz, side)),
            dma((2, nz, side, EARLY)),
            dma((side, nz)),
            dma((side, nz, chunks)),
            dma((nx,)),
            dma((grid_count,)),
            dma,
            dma((7,)),
            dma((row_blocks,)),
            dma((row_blocks,)),
            dma((row_blocks, max(1, nx - 1))),
            dma((row_blocks, max(1, nx - 1))),
            dma((row_blocks, grid_count)),
            dma((row_blocks, grid_count)),
            dma((tile_count,)),
            dma((tile_count,)),
            dma((tile_count,)),
            dma((tile_count,)),
            dma((grid_count,)),
            dma((grid_count,)),
        ],
        compiler_params=pltpu.CompilerParams(
            collective_id=0, has_side_effects=True, vmem_limit_bytes=VMEM_LIMIT
        ),
    )(
        sig_blocks,
        domain_blocks,
        point_values,
        density,
        coulomb_core,
        screen_mask,
        ao_centers,
        ao_widths.reshape(1, total),
        point_coords,
        lmo_coeffs,
    )


def solution(mesh):
    in_specs = (
        P("grid", "tile"),
        P("grid", None),
        P("grid", "tile"),
        P(),
        P(),
        P(),
        P(),
        P(None, "grid"),
        P("tile", None),
        P(),
    )
    out_specs = P("tile", "grid")
    return jax.shard_map(shards, mesh=mesh, in_specs=in_specs, out_specs=out_specs, check_vma=False)
```

```python
import functools
import math

import jax
import jax.numpy as jnp
from jax import lax
from jax.experimental import pallas as pl
from jax.experimental.pallas import tpu as pltpu
from jax.sharding import PartitionSpec as P

MESH = pl.DeviceIdType.MESH
VMEM_LIMIT = 48 * 1024 * 1024
CHUNK = 512
LAG = 3
f32 = jnp.float32
bf16 = jnp.bfloat16
NT = (((1,), (1,)), ((), ()))
TN = (((0,), (0,)), ((), ()))


def grid_split(grid_count):
    inner = max(1, math.isqrt(max(1, grid_count // 2)))
    while grid_count % inner:
        inner -= 1
    return grid_count // inner, inner


def column_cuts(cols):
    early = max(128, cols * 5 // 32 // 128 * 128)
    cuts = [(start, min(CHUNK, cols - early - start)) for start in range(0, cols - early, CHUNK)]
    return cuts + [(cols - early, early)]


def remote(src, dst, send_sem, recv_sem, device):
    return pltpu.make_async_remote_copy(
        src_ref=src,
        dst_ref=dst,
        send_sem=send_sem,
        recv_sem=recv_sem,
        device_id=device,
        device_id_type=MESH,
    )


def listed(table_ref, row, block_id):
    flag = jnp.float32(0.0)
    for i in range(table_ref.shape[1]):
        flag = jnp.where(table_ref[row, i] == block_id, jnp.float32(1.0), flag)
    return flag


def dot(a, b, dims=(((1,), (0,)), ((), ()))):
    return lax.dot_general(a, b, dims, preferred_element_type=f32)


def kernel(
    nz,
    ny,
    nx,
    sig_ref,
    domain_ref,
    value_ref,
    density_hbm,
    core_hbm,
    mask_hbm,
    centers_hbm,
    widths_hbm,
    coords_hbm,
    lmo_hbm,
    out_ref,
    all_ref,
    density_ref,
    acc_ref,
    part_ref,
    sibling_ref,
    pair_ref,
    peer_ref,
    total_ref,
    back_ref,
    core_ref,
    mask_ref,
    centers_ref,
    widths_ref,
    coords_ref,
    lmo_ref,
    scaled_ref,
    spread_ref,
    weighted_ref,
    pot_ref,
    got_ref,
    flat_ref,
    send_ref,
    share_ref,
    own_ref,
    weights_ref,
    rows_ref,
    flags_ref,
    half_ref,
    product_ref,
    zs,
    zr,
    ds_,
    dr,
    ys,
    ye,
    yl,
    yt,
    es,
    er,
    local_sem,
    load_sem,
    cs,
    cr,
    xs,
    xr,
    gs,
    gr,
    vs,
    vr,
    ws,
    wr,
    fs,
    fr,
):
    grid_count, tile_count, nc = nz * ny, nx * 2, 2
    batch, cols = value_ref.shape
    rows = density_ref.shape[0]
    block = core_ref.shape[0]
    blocks = mask_ref.shape[0]
    slab = batch // tile_count
    tile_blocks = cols // block
    row_blocks = rows // block
    cuts = column_cuts(cols)
    chunks = len(cuts)
    early = cuts[-1][1]
    tip = chunks - 1
    strips = domain_ref.shape[0]
    strip_width = lmo_ref.shape[1] // strips
    per_tile = strips // tile_count

    g, t = lax.axis_index("grid"), lax.axis_index("tile")
    z, y = g // ny, g % ny
    x, c = t // nc, t % nc
    place = c * nx + x
    has_left, has_right = z > 0, z < nz - 1
    left = (lax.rem(z + nz - 1, nz) * ny + y, t)
    right = (lax.rem(z + 1, nz) * ny + y, t)
    y_peers = [(z * ny + lax.rem(y + d, ny), t) for d in range(1, ny)]
    x_peers = [(g, lax.rem(x + d, nx) * nc + c) for d in range(1, nx)]
    sibling = (g, x * nc + (1 - c))
    far_tiles = [
        lax.rem(x + d, nx) * nc + (c if e == 0 else 1 - c) for d in range(1, nx) for e in range(nc)
    ]
    tile_order = far_tiles + [x * nc + (1 - c), t]

    loads = [
        pltpu.make_async_copy(src, dst, load_sem.at[i])
        for i, (src, dst) in enumerate(
            [
                (coords_hbm, coords_ref),
                (widths_hbm, widths_ref),
                (centers_hbm, centers_ref),
                (mask_hbm, mask_ref),
                (core_hbm, core_ref),
                (density_hbm, density_ref),
                (lmo_hbm, lmo_ref),
            ]
        )
    ]
    small_loads, core_load, density_load, lmo_load = loads[:4], loads[4], loads[5], loads[6]

    barrier = pltpu.get_barrier_semaphore()

    def hello(device):
        pl.semaphore_signal(barrier, inc=1, device_id=device, device_id_type=MESH)

    @pl.when(has_left)
    def _():
        hello(left)

    @pl.when(has_right)
    def _():
        hello(right)

    for peer in y_peers + [(g, tile) for tile in tile_order[:-1]]:
        hello(peer)

    for m in range(tile_blocks):
        lanes = slice(m * block, (m + 1) * block)
        flag = listed(sig_ref, 0, t * tile_blocks + m)
        all_ref[g, :, lanes] = (value_ref[:, lanes].astype(f32) * flag).astype(bf16)

    neighbours = (
        ny - 1 + tile_count - 1 + jnp.where(has_left, 1, 0) + jnp.where(has_right, 1, 0)
    )
    pl.semaphore_wait(barrier, neighbours)

    def source(line, d):
        return line * ny + lax.rem(y + ny - d, ny)

    def piece(src, q):
        return all_ref.at[src, :, pl.ds(*cuts[q])]

    def z_sems(lane, line, d, q):
        slot = line - lane
        if d == 0:
            return zs.at[lane, line], zr.at[slot, q]
        return ds_.at[lane, line, d - 1], dr.at[slot, d - 1]

    def along(line, d, q, lane):
        spot = piece(source(line, d), q)
        send, recv = z_sems(lane, line, d, q)
        return remote(spot, spot, send, recv, left if lane else right)

    def across(line, d, q, sems):
        spot = piece(source(line, 0), q)
        return remote(spot, spot, *sems, y_peers[d - 1])

    def along_arrived(line, d, q, lane):
        spot = piece(source(line, d), q)
        send, recv = z_sems(lane, line, d, q)
        remote(spot, spot, send, recv, right).wait_recv()

    def arrived(spot, recv):
        remote(spot, spot, ys.at[0, 0], recv, right).wait_recv()

    def both_ways(d, q):
        @pl.when(has_right)
        def _():
            along(z, d, q, 0).start()

        @pl.when(has_left)
        def _():
            along(z, d, q, 1).start()

    half = nz // 2

    def send_across(i, line, q):
        if q != tip:
            for d in range(1, ny):
                recv = ye.at[d - 1, i] if i < half else yl.at[d - 1, q]
                across(line, d, q, (ys.at[d - 1, i], recv)).start()

    for d in range(1, ny):
        across(z, d, tip, (ys.at[d - 1, nz], yt.at[d - 1])).start()
    for q in range(chunks):
        both_ways(0, q)
        send_across(0, z, q)
    for load in loads:
        load.start()

    for load in small_loads:
        load.wait()
    point = lax.broadcasted_iota(jnp.int32, (slab, batch), 1)
    wanted = lax.broadcasted_iota(jnp.int32, (slab, batch), 0) + place * slab
    here = [
        jnp.sum(
            jnp.where(point == wanted, coords_ref[d : d + 1, :], 0.0), axis=1, keepdims=True
        )
        for d in range(3)
    ]
    for j in range(blocks):
        lanes = slice(j * block, (j + 1) * block)
        distance = None
        for d in range(3):
            offset = centers_ref[d : d + 1, lanes] - here[d]
            distance = offset * offset if distance is None else distance + offset * offset
        coefficient = 1.0 / jnp.sqrt(distance + widths_ref[0:1, lanes])
        scaled_ref[j * slab : (j + 1) * slab, :] = coefficient * listed(sig_ref, 0, j)

    for d in range(1, ny):
        arrived(piece(source(z, d), tip), yt.at[d - 1])
        both_ways(d, tip)

    total_rows = blocks * slab
    row = lax.broadcasted_iota(jnp.int32, (total_rows, blocks), 0)
    first = lax.broadcasted_iota(jnp.int32, (total_rows, blocks), 1) * slab
    expand = jnp.where((row >= first) & (row < first + slab), 1.0, 0.0).astype(bf16)
    screen = mask_ref[...].astype(f32).astype(bf16)
    spread = dot(dot(expand, screen).astype(bf16), expand, NT)
    row = lax.broadcasted_iota(jnp.int32, (total_rows, total_rows), 0)
    column = lax.broadcasted_iota(jnp.int32, (total_rows, total_rows), 1)
    spread_ref[...] = jnp.where(
        lax.rem(row, slab) == lax.rem(column, slab), spread, 0.0
    ).astype(bf16)
    for s in range(strips):
        for m in range(tile_blocks):
            flags_ref[s, m] = listed(domain_ref, s, t * tile_blocks + m)

    near = jnp.minimum(z, nz - 1 - z)

    def nearest(i):
        step = (i + 1) // 2 if i % 2 else -(i // 2)
        low = z < nz - 1 - z
        paired = jnp.where(low, z + step, z - step)
        single = jnp.where(low, i, nz - 1 - i)
        return jnp.where(i <= 2 * near, paired, single)

    order = [nearest(i) for i in range(nz)]

    row_start = pl.multiple_of((g * rows) % cols, rows)
    owner = (g * rows) // cols
    is_owner = owner == t
    in_column = owner % nc == c

    def share(line, d):
        src = source(line, d)

        @pl.when(is_owner)
        def _():
            for i, peer in enumerate(x_peers + [sibling]):
                remote(
                    all_ref.at[src, :, pl.ds(row_start, rows)],
                    rows_ref.at[src],
                    es.at[i],
                    er.at[src],
                    peer,
                ).start()

    def take_across(i):
        for d in range(1, ny):
            arrived(all_ref.at[0, :, pl.ds(0, cols - early)], ye.at[d - 1, i])
            share(order[i], d)

    def serve(step, q, sources):
        for lane, line, here_, onward in (
            (0, z - step, z >= step, has_right),
            (1, z + step, z + step <= nz - 1, has_left),
        ):

            @pl.when(here_)
            def _():
                for d in sources:
                    along_arrived(line, d, q, lane)

                    @pl.when(onward)
                    def _():
                        along(line, d, q, lane).start()

    members = [source(order[i], d) for i in range(nz) for d in range(ny)]
    size = half * ny
    groups = (members[:size], members[size:])

    def gathered(group, start, width):
        return jnp.concatenate(
            [all_ref[src, :, start : start + width] for src in groups[group]], axis=0
        )

    def multiply(q):
        start, width = cuts[q]
        if q != tip:
            for d in range(1, ny):
                arrived(all_ref.at[pl.ds(0, nz - half), :, pl.ds(start, width)], yl.at[d - 1, q])
        values = gathered(1, start, width)
        for i in range(row_blocks):
            lanes = slice(i * block, (i + 1) * block)
            value = dot(values, density_ref[lanes, start : start + width], NT)
            if q:
                value = acc_ref[:, lanes] + value
            if q == tip:
                store_part(1, i, value)
                core_copy(1, i).start()
                if i > 0:
                    exchange(1, i - 1)
            else:
                acc_ref[:, lanes] = value

    def store_part(group, i, value):
        if slab % 8 == 0:
            split = value.reshape(size, nc, nx, slab, block).astype(bf16)
            for e in range(nc):
                for h in range(nx):
                    part_ref[group, i, e, h] = split[:, e, h]
        else:
            for n in range(size):
                for e in range(nc):
                    for h in range(nx):
                        first = ((n * nc + e) * nx + h) * slab
                        part_ref[group, i, e, h, n] = value[first : first + slab].astype(bf16)

    def core_copy(group, i):
        return remote(
            part_ref.at[group, i, 1 - c], sibling_ref.at[group, i], cs, cr.at[group, i], sibling
        )

    def pair_copy(group, i, d):
        return remote(
            pair_ref.at[group, i, d - 1],
            peer_ref.at[group, i, d - 1],
            xs.at[d - 1],
            xr.at[group, i, d - 1],
            x_peers[d - 1],
        )

    def exchange(group, i):
        core_copy(group, i).wait_recv()
        for d in range(1, nx):
            column = lax.rem(x + d, nx)
            pair_ref[group, i, d - 1] = (
                part_ref[group, i, c, column].astype(f32)
                + sibling_ref[group, i, column].astype(f32)
            ).astype(bf16)
            pair_copy(group, i, d).start()

    def collect(group, i):
        for d in range(1, nx):
            pair_copy(group, i, d).wait_recv()
        value = part_ref[group, i, c, x].astype(f32) + sibling_ref[group, i, x].astype(f32)
        for d in range(1, nx):
            value = value + peer_ref[group, i, d - 1].astype(f32)
        total_ref[group, i] = value.astype(bf16)
        for n in reversed(range(size)):
            if group or n:
                remote(
                    total_ref.at[group, i, n], back_ref.at[g, i], gs, gr, (groups[group][n], t)
                ).start()
            else:
                back_ref[g, i] = total_ref[group, i, n]

    def part_product(i, late_half):
        middle = cols // 2
        lanes = slice(middle, cols) if late_half else slice(0, middle)
        rows_here = slice(i * block, (i + 1) * block)
        value = dot(
            gathered(0, lanes.start, middle), density_ref[rows_here, lanes], NT
        )
        if not late_half:
            half_ref[...] = value
            return
        store_part(0, i, half_ref[...] + value)
        core_copy(0, i).start()
        if i > 0:
            exchange(0, i - 1)

    def begin():
        density_load.wait()
        for i in range(1, half):
            take_across(i)

    items = [begin]
    for i in range(row_blocks):
        items += [functools.partial(part_product, i, e) for e in range(2)]
    after = [functools.partial(exchange, 0, row_blocks - 1)]
    after += [functools.partial(collect, 0, i) for i in range(row_blocks)]

    def pump(work, count=1):
        for _ in range(min(count, len(work))):
            work.pop(0)()

    done = 0
    share(z, 0)
    for step in range(1, nz):
        for q in range(chunks):
            serve(step, q, (0,))
            send_across(step, order[step], q)
            if (step, q) == (half, chunks // 2 - 1):
                pump(items)
            if (step, q) >= (half, chunks // 2 - 1):
                pump(items)
            if step == nz - 1 and q >= LAG:
                pump(items, len(items))
                multiply(done)
                done += 1
                if q > LAG:
                    pump(after)
        serve(step, tip, range(1, ny))
        if step == 1:
            take_across(0)
        if step < nz - 1:
            share(order[step], 0)
    pump(items, len(items))
    while done < tip:
        multiply(done)
        done += 1
        pump(after)
    pump(after, len(after))
    multiply(tip)
    exchange(1, row_blocks - 1)
    for i in range(row_blocks):
        collect(1, i)

    for i in range(half, nz):
        if i == nz - 1:
            share(order[i], 0)
        for d in range(1, ny):
            share(order[i], d)

    own_rows = pltpu.make_async_copy(
        all_ref.at[:, :, pl.ds(row_start, rows)], rows_ref, local_sem
    )

    @pl.when(is_owner)
    def _():
        own_rows.start()

    core_load.wait()
    def wait_all(spot, recv):
        remote(spot, spot, gs, recv, right).wait_recv()

    wait_all(back_ref.at[pl.ds(0, grid_count - 1)], gr)
    for j in range(blocks):
        span = slice(j * slab, (j + 1) * slab)
        weighted_ref[span, :] = scaled_ref[span, :] * back_ref[
            j // row_blocks, j % row_blocks
        ].astype(f32)
    weighted = weighted_ref[...].astype(bf16)

    tile_rows = tile_blocks * slab
    for n, tile in enumerate(tile_order):
        span = pl.ds(pl.multiple_of(tile * tile_rows, tile_rows), tile_rows)
        screened = dot(spread_ref[span, :], weighted).astype(bf16)
        potential = scaled_ref[span, :] * dot(screened, core_ref[...], NT)
        is_own = n == len(tile_order) - 1
        for m in range(tile_blocks):
            value = potential[m * slab : (m + 1) * slab, :].astype(bf16)
            if is_own:
                got_ref[place, m] = value
            else:
                pot_ref[n, m] = value
        if not is_own:
            remote(
                pot_ref.at[n], got_ref.at[place], vs, vr, (g, tile)
            ).start()

    lmo_load.wait()
    wait_all(got_ref.at[pl.ds(0, tile_count - 1)], vr)
    for i in range(tile_count):
        for m in range(tile_blocks):
            flat_ref[i * slab : (i + 1) * slab, m * block : (m + 1) * block] = got_ref[
                i, m
            ].astype(f32)

    own_total = None
    group_width = nc * per_tile * strip_width
    for n, (d, tiles) in enumerate(
        [(d, tile_order[2 * d - 2 : 2 * d]) for d in range(1, nx)] + [(0, tile_order[-2:])]
    ):
        plane = lax.rem(x + d, nx)
        kept = jnp.concatenate(
            [
                jnp.concatenate(
                    [
                        (
                            flat_ref[:, m * block : (m + 1) * block]
                            * flags_ref[plane * nc * per_tile + k, m]
                        ).astype(bf16)
                        for m in range(tile_blocks)
                    ],
                    axis=1,
                )
                for k in range(nc * per_tile)
            ],
            axis=0,
        )
        start = pl.multiple_of(plane * group_width, group_width)
        values = dot(kept, lmo_ref[:, pl.ds(start, group_width)])
        pieces = []
        for e in range(nc):
            parts = []
            for k in range(e * per_tile, (e + 1) * per_tile):
                parts.append(
                    values[
                        k * batch : (k + 1) * batch, k * strip_width : (k + 1) * strip_width
                    ]
                )
            pieces.append(parts[0] if per_tile == 1 else jnp.concatenate(parts, axis=1))
        for e in range(nc):
            product_ref[n, e] = pieces[e]
        for k, tile in enumerate(tiles):
            index = n * nc + k
            chosen = product_ref[n, lax.rem(tile, nc)]
            if index < tile_count - 1:
                send_ref[index] = chosen.astype(bf16)
                remote(send_ref.at[index], share_ref.at[t], ws, wr, (g, tile)).start()
            else:
                own_total = chosen
    wait_all(share_ref.at[pl.ds(0, tile_count - 1)], wr)
    for tile in tile_order[:-1]:
        own_total = own_total + share_ref[tile].astype(f32)
    own_ref[...] = own_total.astype(bf16)
    for target in reversed(members[1:]):
        remote(own_ref, weights_ref.at[g], fs, fr, (target, t)).start()
    weights_ref[g] = own_ref[...]

    @pl.when(jnp.logical_and(in_column, jnp.logical_not(is_owner)))
    def _():
        for src in range(grid_count):
            spot = rows_ref.at[src]
            pass_on = remote(spot, spot, es.at[nx - 1], er.at[src], sibling)
            pass_on.wait_recv()
            pass_on.start()

    @pl.when(is_owner)
    def _():
        own_rows.wait()

    @pl.when(jnp.logical_not(in_column))
    def _():
        for src in range(grid_count):
            spot = rows_ref.at[src]
            remote(spot, spot, es.at[0], er.at[src], right).wait_recv()

    wait_all(weights_ref.at[pl.ds(0, grid_count - 1)], fr)
    out_ref[...] = dot(
        weights_ref[...].reshape(grid_count * batch, weights_ref.shape[2]),
        rows_ref[...].reshape(grid_count * batch, rows),
        TN,
    ).astype(bf16)

    def drain(ref, sem):
        remote(ref, ref, sem, fr, right).wait_send()

    for line in range(nz):
        for lane, sent in (
            (0, jnp.logical_and(has_right, line <= z)),
            (1, jnp.logical_and(has_left, line >= z)),
        ):

            @pl.when(sent)
            def _():
                drain(all_ref.at[0], zs.at[lane, line])
                for d in range(1, ny):
                    drain(all_ref.at[0, :, pl.ds(cols - early, early)], ds_.at[lane, line, d - 1])

    for d in range(1, ny):
        for i in range(nz):
            drain(all_ref.at[0, :, pl.ds(0, cols - early)], ys.at[d - 1, i])
        drain(all_ref.at[0, :, pl.ds(0, early)], ys.at[d - 1, nz])

    @pl.when(is_owner)
    def _():
        for i in range(nx):
            drain(rows_ref, es.at[i])

    @pl.when(jnp.logical_and(in_column, jnp.logical_not(is_owner)))
    def _():
        drain(rows_ref, es.at[nx - 1])

    drain(sibling_ref, cs)
    for d in range(1, nx):
        drain(pair_ref.at[:, :, d - 1], xs.at[d - 1])
    drain(back_ref.at[pl.ds(0, grid_count - 1)], gs)
    drain(pot_ref, vs)
    drain(send_ref, ws)
    drain(weights_ref.at[pl.ds(0, grid_count - 1)], fs)


def shards(
    point_values,
    sig_blocks,
    density,
    coulomb_core,
    screen_mask,
    ao_centers,
    ao_widths,
    point_coords,
    lmo_coeffs,
    domain_blocks,
):
    grid_count, tile_count = lax.axis_size("grid"), lax.axis_size("tile")
    nz, ny = grid_split(grid_count)
    nc, nx = 2, tile_count // 2
    rows, cols = density.shape
    batch = point_values.shape[0]
    block = coulomb_core.shape[0]
    total = ao_widths.shape[0]
    blocks = total // block
    slab = batch // tile_count
    strip = lmo_coeffs.shape[1] // tile_count
    tile_blocks, row_blocks, chunks = cols // block, rows // block, len(column_cuts(cols))
    dma = pltpu.SemaphoreType.DMA
    smem = pl.BlockSpec(memory_space=pltpu.SMEM)
    vmem = pl.BlockSpec(memory_space=pltpu.VMEM)
    anywhere = pl.BlockSpec(memory_space=pltpu.HBM)
    side = max(1, ny - 1)
    size = nz // 2 * ny
    return pl.pallas_call(
        functools.partial(kernel, nz, ny, nx),
        out_shape=jax.ShapeDtypeStruct((strip, rows), bf16),
        in_specs=[smem, smem, vmem] + [anywhere] * 7,
        out_specs=vmem,
        scratch_shapes=[
            pltpu.VMEM((grid_count, batch, cols), bf16),
            pltpu.VMEM((rows, cols), bf16),
            pltpu.VMEM((size * batch, rows), f32),
            pltpu.VMEM((2, row_blocks, nc, nx, size, slab, block), bf16),
            pltpu.VMEM((2, row_blocks, nx, size, slab, block), bf16),
            pltpu.VMEM((2, row_blocks, max(1, nx - 1), size, slab, block), bf16),
            pltpu.VMEM((2, row_blocks, max(1, nx - 1), size, slab, block), bf16),
            pltpu.VMEM((2, row_blocks, size, slab, block), bf16),
            pltpu.VMEM((grid_count, row_blocks, slab, block), bf16),
            pltpu.VMEM(coulomb_core.shape, bf16),
            pltpu.VMEM(screen_mask.shape, jnp.int32),
            pltpu.VMEM(ao_centers.shape, f32),
            pltpu.VMEM((1, total), f32),
            pltpu.VMEM(point_coords.shape, f32),
            pltpu.VMEM(lmo_coeffs.shape, bf16),
            pltpu.VMEM((blocks * slab, block), f32),
            pltpu.VMEM((blocks * slab, blocks * slab), bf16),
            pltpu.VMEM((blocks * slab, block), f32),
            pltpu.VMEM((tile_count - 1, tile_blocks, slab, block), bf16),
            pltpu.VMEM((tile_count, tile_blocks, slab, block), bf16),
            pltpu.VMEM((batch, cols), f32),
            pltpu.VMEM((tile_count - 1, batch, strip), bf16),
            pltpu.VMEM((tile_count, batch, strip), bf16),
            pltpu.VMEM((batch, strip), bf16),
            pltpu.VMEM((grid_count, batch, strip), bf16),
            pltpu.VMEM((grid_count, batch, rows), bf16),
            pltpu.SMEM((domain_blocks.shape[0], tile_blocks), f32),
            pltpu.VMEM((size * batch, block), f32),
            pltpu.VMEM((nx, nc, batch, strip), f32),
            dma((2, nz)),
            dma((nz - 1, chunks)),
            dma((2, nz, side)),
            dma((nz - 1, side)),
            dma((side, nz + 1)),
            dma((side, nz // 2)),
            dma((side, chunks - 1)),
            dma((side,)),
            dma((nx,)),
            dma((grid_count,)),
            dma,
            dma((7,)),
            dma,
            dma((2, row_blocks)),
            dma((max(1, nx - 1),)),
            dma((2, row_blocks, max(1, nx - 1))),
            dma,
            dma,
            dma,
            dma,
            dma,
            dma,
            dma,
            dma,
        ],
        compiler_params=pltpu.CompilerParams(
            collective_id=0, has_side_effects=True, vmem_limit_bytes=VMEM_LIMIT
        ),
    )(
        *[
            pltpu.with_memory_space_constraint(operand, pltpu.HBM)
            for operand in (
                sig_blocks,
                domain_blocks,
                point_values,
                density,
                coulomb_core,
                screen_mask,
                ao_centers,
                ao_widths.reshape(1, total),
                point_coords,
                lmo_coeffs,
            )
        ]
    )


def solution(mesh):
    in_specs = (
        P("grid", "tile"),
        P("grid", None),
        P("grid", "tile"),
        P(),
        P(),
        P(),
        P(),
        P(None, "grid"),
        P("tile", None),
        P(),
    )
    out_specs = P("tile", "grid")
    return jax.shard_map(shards, mesh=mesh, in_specs=in_specs, out_specs=out_specs, check_vma=False)
```

```python
import functools
import math

import jax
import jax.numpy as jnp
from jax import lax
from jax.experimental import pallas as pl
from jax.experimental.pallas import tpu as pltpu
from jax.sharding import PartitionSpec as P

MESH = pl.DeviceIdType.MESH
VMEM_LIMIT = 48 * 1024 * 1024
CHUNK = 512
FILL = 128
f32 = jnp.float32
bf16 = jnp.bfloat16
NT = (((1,), (1,)), ((), ()))
TN = (((0,), (0,)), ((), ()))


def grid_split(grid_count):
    inner = max(1, math.isqrt(max(1, grid_count // 2)))
    while grid_count % inner:
        inner -= 1
    return grid_count // inner, inner


def column_cuts(cols):
    early = max(128, cols * 4 // 32 // 128 * 128)
    cuts = [(start, min(CHUNK, cols - early - start)) for start in range(0, cols - early, CHUNK)]
    return cuts + [(cols - early, early)]


def remote(src, dst, send_sem, recv_sem, device):
    return pltpu.make_async_remote_copy(
        src_ref=src,
        dst_ref=dst,
        send_sem=send_sem,
        recv_sem=recv_sem,
        device_id=device,
        device_id_type=MESH,
    )


def listed(table_ref, row, block_id):
    flag = jnp.float32(0.0)
    for i in range(table_ref.shape[1]):
        flag = jnp.where(table_ref[row, i] == block_id, jnp.float32(1.0), flag)
    return flag


def dot(a, b, dims=(((1,), (0,)), ((), ()))):
    return lax.dot_general(a, b, dims, preferred_element_type=f32)


def kernel(
    nz,
    ny,
    nx,
    sig_hbm,
    domain_hbm,
    value_hbm,
    density_hbm,
    core_hbm,
    mask_hbm,
    centers_hbm,
    widths_hbm,
    coords_hbm,
    lmo_hbm,
    out_ref,
    sig_ref,
    domain_ref,
    value_ref,
    all_ref,
    stage_ref,
    turned_ref,
    acc_ref,
    part_ref,
    sibling_ref,
    pair_ref,
    peer_ref,
    total_ref,
    back_ref,
    core_ref,
    mask_ref,
    centers_ref,
    widths_ref,
    coords_ref,
    lmo_ref,
    scaled_ref,
    spread_ref,
    weighted_ref,
    pot_ref,
    got_ref,
    flat_ref,
    send_ref,
    share_ref,
    own_ref,
    weights_ref,
    rows_ref,
    flags_ref,
    product_ref,
    zs,
    zr,
    ds_,
    dr,
    ys,
    ye,
    yl,
    yt,
    es,
    er,
    local_sem,
    load_sem,
    cs,
    cr,
    xs,
    xr,
    gs,
    gr,
    vs,
    vr,
    ws,
    wr,
    fs,
    fr,
):
    grid_count, tile_count, nc = nz * ny, nx * 2, 2
    batch, cols = value_ref.shape
    rows = turned_ref.shape[1]
    block = core_ref.shape[0]
    blocks = mask_ref.shape[0]
    slab = batch // tile_count
    tile_blocks = cols // block
    row_blocks = rows // block
    cuts = column_cuts(cols)
    chunks = len(cuts)
    early = cuts[-1][1]
    tip = chunks - 1
    strips = domain_ref.shape[0]
    strip_width = lmo_ref.shape[1] // strips
    per_tile = strips // tile_count

    g, t = lax.axis_index("grid"), lax.axis_index("tile")
    z, y = g // ny, g % ny
    x, c = t // nc, t % nc
    place = c * nx + x
    has_left, has_right = z > 0, z < nz - 1
    left = (lax.rem(z + nz - 1, nz) * ny + y, t)
    right = (lax.rem(z + 1, nz) * ny + y, t)
    y_peers = [(z * ny + lax.rem(y + d, ny), t) for d in range(1, ny)]
    x_peers = [(g, lax.rem(x + d, nx) * nc + c) for d in range(1, nx)]
    sibling = (g, x * nc + (1 - c))
    far_tiles = [
        lax.rem(x + d, nx) * nc + (c if e == 0 else 1 - c) for d in range(1, nx) for e in range(nc)
    ]
    tile_order = far_tiles + [x * nc + (1 - c), t]

    small_loads = [
        pltpu.make_async_copy(src, dst, load_sem.at[i])
        for i, (src, dst) in enumerate(
            [
                (sig_hbm, sig_ref),
                (value_hbm, value_ref),
                (domain_hbm, domain_ref),
                (coords_hbm, coords_ref),
                (widths_hbm, widths_ref),
                (centers_hbm, centers_ref),
                (mask_hbm, mask_ref),
                (core_hbm, core_ref),
                (lmo_hbm, lmo_ref),
            ]
        )
    ]
    core_load, lmo_load = small_loads[7:]
    first_loads, small_loads = small_loads[:2], small_loads[2:7]

    def stage_load(i):
        return pltpu.make_async_copy(
            density_hbm.at[pl.ds(i * block, block)], stage_ref.at[i % 2], load_sem.at[9 + i % 2]
        )

    for load in first_loads + small_loads:
        load.start()
    for i in range(min(2, row_blocks)):
        stage_load(i).start()
    core_load.start()

    barrier = pltpu.get_barrier_semaphore()

    def hello(device):
        pl.semaphore_signal(barrier, inc=1, device_id=device, device_id_type=MESH)

    @pl.when(has_left)
    def _():
        hello(left)

    @pl.when(has_right)
    def _():
        hello(right)

    for peer in y_peers + [(g, tile) for tile in tile_order[:-1]]:
        hello(peer)

    for load in first_loads:
        load.wait()
    for m in range(tile_blocks):
        lanes = slice(m * block, (m + 1) * block)
        flag = listed(sig_ref, 0, t * tile_blocks + m)
        all_ref[g, :, lanes] = (value_ref[:, lanes].astype(f32) * flag).astype(bf16)

    neighbours = (
        ny - 1 + tile_count - 1 + jnp.where(has_left, 1, 0) + jnp.where(has_right, 1, 0)
    )
    pl.semaphore_wait(barrier, neighbours)

    def source(line, d):
        return line * ny + lax.rem(y + ny - d, ny)

    def piece(src, q):
        return all_ref.at[src, :, pl.ds(*cuts[q])]

    def z_sems(lane, line, d, q):
        slot = line - lane
        if d == 0:
            return zs.at[lane, line], zr.at[slot, q]
        return ds_.at[lane, line, d - 1], dr.at[slot, d - 1]

    def along(line, d, q, lane):
        spot = piece(source(line, d), q)
        send, recv = z_sems(lane, line, d, q)
        return remote(spot, spot, send, recv, left if lane else right)

    def across(line, d, q, sems):
        spot = piece(source(line, 0), q)
        return remote(spot, spot, *sems, y_peers[d - 1])

    def along_arrived(line, d, q, lane):
        spot = piece(source(line, d), q)
        send, recv = z_sems(lane, line, d, q)
        remote(spot, spot, send, recv, right).wait_recv()

    def arrived(spot, recv):
        remote(spot, spot, ys.at[0, 0], recv, right).wait_recv()

    def both_ways(d, q):
        @pl.when(has_right)
        def _():
            along(z, d, q, 0).start()

        @pl.when(has_left)
        def _():
            along(z, d, q, 1).start()

    half = nz // 2

    def send_across(i, line, q):
        if q != tip:
            for d in range(1, ny):
                recv = ye.at[d - 1, i] if i < nz - 1 else yl.at[d - 1, q]
                across(line, d, q, (ys.at[d - 1, i], recv)).start()

    for d in range(1, ny):
        across(z, d, tip, (ys.at[d - 1, nz], yt.at[d - 1])).start()
    for q in range(chunks):
        both_ways(0, q)
        send_across(0, z, q)
    def turn(i, k):
        if k == 0:
            stage_load(i).wait()
        lanes = slice(k * block, (k + 1) * block)
        turned_ref[lanes, i * block : (i + 1) * block] = stage_ref[i % 2, :, lanes].T
        if k == tile_blocks - 1:
            if i + 2 < row_blocks:
                stage_load(i + 2).start()
            if i == row_blocks - 1:
                lmo_load.start()

    turns = [functools.partial(turn, i, k) for i in range(row_blocks) for k in range(tile_blocks)]

    def pump(work, count=1):
        for _ in range(min(count, len(work))):
            work.pop(0)()

    for load in small_loads:
        load.wait()
    point = lax.broadcasted_iota(jnp.int32, (slab, batch), 1)
    wanted = lax.broadcasted_iota(jnp.int32, (slab, batch), 0) + place * slab
    here = [
        jnp.sum(
            jnp.where(point == wanted, coords_ref[d : d + 1, :], 0.0), axis=1, keepdims=True
        )
        for d in range(3)
    ]
    for j in range(blocks):
        lanes = slice(j * block, (j + 1) * block)
        distance = None
        for d in range(3):
            offset = centers_ref[d : d + 1, lanes] - here[d]
            distance = offset * offset if distance is None else distance + offset * offset
        coefficient = 1.0 / jnp.sqrt(distance + widths_ref[0:1, lanes])
        scaled_ref[j * slab : (j + 1) * slab, :] = coefficient * listed(sig_ref, 0, j)

    pump(turns, tile_blocks)
    for d in range(1, ny):
        arrived(piece(source(z, d), tip), yt.at[d - 1])
        both_ways(d, tip)

    total_rows = blocks * slab
    row = lax.broadcasted_iota(jnp.int32, (total_rows, blocks), 0)
    first = lax.broadcasted_iota(jnp.int32, (total_rows, blocks), 1) * slab
    expand = jnp.where((row >= first) & (row < first + slab), 1.0, 0.0).astype(bf16)
    screen = mask_ref[...].astype(f32).astype(bf16)
    spread = dot(dot(expand, screen).astype(bf16), expand, NT)
    row = lax.broadcasted_iota(jnp.int32, (total_rows, total_rows), 0)
    column = lax.broadcasted_iota(jnp.int32, (total_rows, total_rows), 1)
    spread_ref[...] = jnp.where(
        lax.rem(row, slab) == lax.rem(column, slab), spread, 0.0
    ).astype(bf16)
    for s in range(strips):
        for m in range(tile_blocks):
            flags_ref[s, m] = listed(domain_ref, s, t * tile_blocks + m)

    near = jnp.minimum(z, nz - 1 - z)

    def nearest(i):
        step = (i + 1) // 2 if i % 2 else -(i // 2)
        low = z < nz - 1 - z
        paired = jnp.where(low, z + step, z - step)
        single = jnp.where(low, i, nz - 1 - i)
        return jnp.where(i <= 2 * near, paired, single)

    order = [nearest(i) for i in range(nz)]

    row_start = pl.multiple_of((g * rows) % cols, rows)
    owner = (g * rows) // cols
    is_owner = owner == t
    in_column = owner % nc == c

    def share(line, d):
        src = source(line, d)

        @pl.when(is_owner)
        def _():
            for i, peer in enumerate(x_peers + [sibling]):
                remote(
                    all_ref.at[src, :, pl.ds(row_start, rows)],
                    rows_ref.at[src],
                    es.at[i],
                    er.at[src],
                    peer,
                ).start()

    def take_across(i):
        for d in range(1, ny):
            arrived(all_ref.at[0, :, pl.ds(0, cols - early)], ye.at[d - 1, i])
            share(order[i], d)

    def serve(step, q, sources):
        for lane, line, here_, onward in (
            (0, z - step, z >= step, has_right),
            (1, z + step, z + step <= nz - 1, has_left),
        ):

            @pl.when(here_)
            def _():
                for d in sources:
                    along_arrived(line, d, q, lane)

                    @pl.when(onward)
                    def _():
                        along(line, d, q, lane).start()

    members = [source(order[i], d) for i in range(nz) for d in range(ny)]
    lines = [list(range(half))] + [[i] for i in range(half, nz)]
    spans = [(group[0] * ny, (group[-1] + 1) * ny) for group in lines]
    final = len(lines) - 1

    def gathered(group, start, width):
        first, stop = spans[group]
        sources = members[first:stop]
        if group != final:
            sources = sources * max(1, FILL // ((stop - first) * batch))
        return jnp.concatenate(
            [all_ref[src, :, start : start + width] for src in sources], axis=0
        )

    def multiply(q):
        start, width = cuts[q]
        if q != tip:
            for d in range(1, ny):
                arrived(piece(0, q), yl.at[d - 1, q])
        values = gathered(final, start, width)
        for i in range(row_blocks):
            lanes = slice(i * block, (i + 1) * block)
            value = dot(values, turned_ref[start : start + width, lanes])
            if q:
                value = acc_ref[:, lanes] + value
            if q == tip:
                store_part(final, i, value)
            else:
                acc_ref[:, lanes] = value

    def store_part(group, i, value):
        first, stop = spans[group]
        size = stop - first
        value = value[: size * batch]
        if slab % 8 == 0:
            split = value.reshape(size, nc, nx, slab, block).astype(bf16)
            for e in range(nc):
                for h in range(nx):
                    part_ref[i, e, h, first:stop] = split[:, e, h]
        else:
            for n in range(size):
                for e in range(nc):
                    for h in range(nx):
                        row = ((n * nc + e) * nx + h) * slab
                        part_ref[i, e, h, first + n] = value[row : row + slab].astype(bf16)
        core_copy(group, i).start()

    def span_of(group):
        first, stop = spans[group]
        return pl.ds(first, stop - first)

    def core_copy(group, i):
        span = span_of(group)
        return remote(
            part_ref.at[i, 1 - c, :, span],
            sibling_ref.at[i, :, span],
            cs,
            cr.at[group, i],
            sibling,
        )

    def pair_copy(group, i, d):
        span = span_of(group)
        return remote(
            pair_ref.at[i, d - 1, span],
            peer_ref.at[i, d - 1, span],
            xs.at[d - 1],
            xr.at[group, i, d - 1],
            x_peers[d - 1],
        )

    def exchange(group, i):
        span = slice(*spans[group])
        core_copy(group, i).wait_recv()
        for d in range(1, nx):
            column = lax.rem(x + d, nx)
            pair_ref[i, d - 1, span] = (
                part_ref[i, c, column, span].astype(f32)
                + sibling_ref[i, column, span].astype(f32)
            ).astype(bf16)
            pair_copy(group, i, d).start()

    def collect(group, i):
        first, stop = spans[group]
        span = slice(first, stop)
        for d in range(1, nx):
            pair_copy(group, i, d).wait_recv()
        value = part_ref[i, c, x, span].astype(f32) + sibling_ref[i, x, span].astype(f32)
        for d in range(1, nx):
            value = value + peer_ref[i, d - 1, span].astype(f32)
        total_ref[i, span] = value.astype(bf16)
        for n in reversed(range(first, stop)):
            if n:
                remote(
                    total_ref.at[i, n], back_ref.at[g, i], gs, gr, (members[n], t)
                ).start()
            else:
                back_ref[g, i] = total_ref[i, n]

    def group_product(group, i):
        if i == 0:
            for line in lines[group]:
                if line:
                    take_across(line)
        store_part(
            group,
            i,
            dot(
                gathered(group, 0, cols), turned_ref[:, i * block : (i + 1) * block]
            ),
        )
        if i > 1:
            exchange(group, i - 2)

    items, after = [], []

    def enqueue(group):
        items.extend(functools.partial(group_product, group, i) for i in range(row_blocks))
        for i in range(max(0, row_blocks - 2), row_blocks):
            items.append(functools.partial(exchange, group, i))
        after.extend(functools.partial(collect, group, i) for i in range(row_blocks))

    share(z, 0)
    for step in range(1, nz):
        for q in range(chunks):
            serve(step, q, (0,))
            send_across(step, order[step], q)
            pump(turns, 3)
            if (step, q) == (half, chunks // 2 + 1):
                pump(turns, len(turns))
                enqueue(0)
            if half < step and q == 2:
                enqueue(step - half)
            if step == nz - 1 and q >= 4:
                pump(after)
            pump(items)
        serve(step, tip, range(1, ny))
        if step == 1:
            take_across(0)
        if step < nz - 1:
            share(order[step], 0)
    pump(items, len(items))
    for q in range(chunks):
        multiply(q)
    for i in range(row_blocks):
        exchange(final, i)
    pump(after, len(after))
    for i in range(row_blocks):
        collect(final, i)

    for d in range(ny):
        share(order[nz - 1], d)

    own_rows = pltpu.make_async_copy(
        all_ref.at[:, :, pl.ds(row_start, rows)], rows_ref, local_sem
    )

    @pl.when(is_owner)
    def _():
        own_rows.start()

    core_load.wait()
    def wait_all(spot, recv):
        remote(spot, spot, gs, recv, right).wait_recv()

    wait_all(back_ref.at[pl.ds(0, grid_count - 1)], gr)
    for j in range(blocks):
        span = slice(j * slab, (j + 1) * slab)
        weighted_ref[span, :] = scaled_ref[span, :] * back_ref[
            j // row_blocks, j % row_blocks
        ].astype(f32)
    weighted = weighted_ref[...].astype(bf16)

    tile_rows = tile_blocks * slab
    for n, tile in enumerate(tile_order):
        span = pl.ds(pl.multiple_of(tile * tile_rows, tile_rows), tile_rows)
        screened = dot(spread_ref[span, :], weighted).astype(bf16)
        potential = scaled_ref[span, :] * dot(screened, core_ref[...], NT)
        is_own = n == len(tile_order) - 1
        for m in range(tile_blocks):
            value = potential[m * slab : (m + 1) * slab, :].astype(bf16)
            if is_own:
                got_ref[place, m] = value
            else:
                pot_ref[n, m] = value
        if not is_own:
            remote(
                pot_ref.at[n], got_ref.at[place], vs, vr, (g, tile)
            ).start()

    lmo_load.wait()
    wait_all(got_ref.at[pl.ds(0, tile_count - 1)], vr)
    for i in range(tile_count):
        for m in range(tile_blocks):
            flat_ref[i * slab : (i + 1) * slab, m * block : (m + 1) * block] = got_ref[
                i, m
            ].astype(f32)

    own_total = None
    group_width = nc * per_tile * strip_width
    for n, (d, tiles) in enumerate(
        [(d, tile_order[2 * d - 2 : 2 * d]) for d in range(1, nx)] + [(0, tile_order[-2:])]
    ):
        plane = lax.rem(x + d, nx)
        kept = jnp.concatenate(
            [
                jnp.concatenate(
                    [
                        (
                            flat_ref[:, m * block : (m + 1) * block]
                            * flags_ref[plane * nc * per_tile + k, m]
                        ).astype(bf16)
                        for m in range(tile_blocks)
                    ],
                    axis=1,
                )
                for k in range(nc * per_tile)
            ],
            axis=0,
        )
        start = pl.multiple_of(plane * group_width, group_width)
        values = dot(kept, lmo_ref[:, pl.ds(start, group_width)])
        pieces = []
        for e in range(nc):
            parts = []
            for k in range(e * per_tile, (e + 1) * per_tile):
                parts.append(
                    values[
                        k * batch : (k + 1) * batch, k * strip_width : (k + 1) * strip_width
                    ]
                )
            pieces.append(parts[0] if per_tile == 1 else jnp.concatenate(parts, axis=1))
        for e in range(nc):
            product_ref[n, e] = pieces[e]
        for k, tile in enumerate(tiles):
            index = n * nc + k
            chosen = product_ref[n, lax.rem(tile, nc)]
            if index < tile_count - 1:
                send_ref[index] = chosen.astype(bf16)
                remote(send_ref.at[index], share_ref.at[t], ws, wr, (g, tile)).start()
            else:
                own_total = chosen
    wait_all(share_ref.at[pl.ds(0, tile_count - 1)], wr)
    for tile in tile_order[:-1]:
        own_total = own_total + share_ref[tile].astype(f32)
    own_ref[...] = own_total.astype(bf16)
    for target in reversed(members[1:]):
        remote(own_ref, weights_ref.at[g], fs, fr, (target, t)).start()
    weights_ref[g] = own_ref[...]

    @pl.when(jnp.logical_and(in_column, jnp.logical_not(is_owner)))
    def _():
        for src in range(grid_count):
            spot = rows_ref.at[src]
            pass_on = remote(spot, spot, es.at[nx - 1], er.at[src], sibling)
            pass_on.wait_recv()
            pass_on.start()

    @pl.when(is_owner)
    def _():
        own_rows.wait()

    @pl.when(jnp.logical_not(in_column))
    def _():
        for src in range(grid_count):
            spot = rows_ref.at[src]
            remote(spot, spot, es.at[0], er.at[src], right).wait_recv()

    wait_all(weights_ref.at[pl.ds(0, grid_count - 1)], fr)
    out_ref[...] = dot(
        weights_ref[...].reshape(grid_count * batch, weights_ref.shape[2]),
        rows_ref[...].reshape(grid_count * batch, rows),
        TN,
    ).astype(bf16)

    def drain(ref, sem):
        remote(ref, ref, sem, fr, right).wait_send()

    for line in range(nz):
        for lane, sent in (
            (0, jnp.logical_and(has_right, line <= z)),
            (1, jnp.logical_and(has_left, line >= z)),
        ):

            @pl.when(sent)
            def _():
                drain(all_ref.at[0], zs.at[lane, line])
                for d in range(1, ny):
                    drain(all_ref.at[0, :, pl.ds(cols - early, early)], ds_.at[lane, line, d - 1])

    for d in range(1, ny):
        for i in range(nz):
            drain(all_ref.at[0, :, pl.ds(0, cols - early)], ys.at[d - 1, i])
        drain(all_ref.at[0, :, pl.ds(0, early)], ys.at[d - 1, nz])

    @pl.when(is_owner)
    def _():
        for i in range(nx):
            drain(rows_ref, es.at[i])

    @pl.when(jnp.logical_and(in_column, jnp.logical_not(is_owner)))
    def _():
        drain(rows_ref, es.at[nx - 1])

    drain(sibling_ref, cs)
    for d in range(1, nx):
        drain(pair_ref.at[:, d - 1], xs.at[d - 1])
    drain(back_ref.at[pl.ds(0, grid_count - 1)], gs)
    drain(pot_ref, vs)
    drain(send_ref, ws)
    drain(weights_ref.at[pl.ds(0, grid_count - 1)], fs)


def shards(
    point_values,
    sig_blocks,
    density,
    coulomb_core,
    screen_mask,
    ao_centers,
    ao_widths,
    point_coords,
    lmo_coeffs,
    domain_blocks,
):
    grid_count, tile_count = lax.axis_size("grid"), lax.axis_size("tile")
    nz, ny = grid_split(grid_count)
    nc, nx = 2, tile_count // 2
    rows, cols = density.shape
    batch = point_values.shape[0]
    block = coulomb_core.shape[0]
    total = ao_widths.shape[0]
    blocks = total // block
    slab = batch // tile_count
    strip = lmo_coeffs.shape[1] // tile_count
    tile_blocks, row_blocks, chunks = cols // block, rows // block, len(column_cuts(cols))
    dma = pltpu.SemaphoreType.DMA
    vmem = pl.BlockSpec(memory_space=pltpu.VMEM)
    anywhere = pl.BlockSpec(memory_space=pltpu.HBM)
    side = max(1, ny - 1)
    groups = 1 + nz - nz // 2
    return pl.pallas_call(
        functools.partial(kernel, nz, ny, nx),
        out_shape=jax.ShapeDtypeStruct((strip, rows), bf16),
        in_specs=[anywhere] * 10,
        out_specs=vmem,
        scratch_shapes=[
            pltpu.SMEM(sig_blocks.shape, jnp.int32),
            pltpu.SMEM(domain_blocks.shape, jnp.int32),
            pltpu.VMEM((batch, cols), bf16),
            pltpu.VMEM((grid_count, batch, cols), bf16),
            pltpu.VMEM((2, block, cols), bf16),
            pltpu.VMEM((cols, rows), bf16),
            pltpu.VMEM((ny * batch, rows), f32),
            pltpu.VMEM((row_blocks, nc, nx, grid_count, slab, block), bf16),
            pltpu.VMEM((row_blocks, nx, grid_count, slab, block), bf16),
            pltpu.VMEM((row_blocks, max(1, nx - 1), grid_count, slab, block), bf16),
            pltpu.VMEM((row_blocks, max(1, nx - 1), grid_count, slab, block), bf16),
            pltpu.VMEM((row_blocks, grid_count, slab, block), bf16),
            pltpu.VMEM((grid_count, row_blocks, slab, block), bf16),
            pltpu.VMEM(coulomb_core.shape, bf16),
            pltpu.VMEM(screen_mask.shape, jnp.int32),
            pltpu.VMEM(ao_centers.shape, f32),
            pltpu.VMEM((1, total), f32),
            pltpu.VMEM(point_coords.shape, f32),
            pltpu.VMEM(lmo_coeffs.shape, bf16),
            pltpu.VMEM((blocks * slab, block), f32),
            pltpu.VMEM((blocks * slab, blocks * slab), bf16),
            pltpu.VMEM((blocks * slab, block), f32),
            pltpu.VMEM((tile_count - 1, tile_blocks, slab, block), bf16),
            pltpu.VMEM((tile_count, tile_blocks, slab, block), bf16),
            pltpu.VMEM((batch, cols), f32),
            pltpu.VMEM((tile_count - 1, batch, strip), bf16),
            pltpu.VMEM((tile_count, batch, strip), bf16),
            pltpu.VMEM((batch, strip), bf16),
            pltpu.VMEM((grid_count, batch, strip), bf16),
            pltpu.VMEM((grid_count, batch, rows), bf16),
            pltpu.SMEM((domain_blocks.shape[0], tile_blocks), f32),
            pltpu.VMEM((nx, nc, batch, strip), f32),
            dma((2, nz)),
            dma((nz - 1, chunks)),
            dma((2, nz, side)),
            dma((nz - 1, side)),
            dma((side, nz + 1)),
            dma((side, nz - 1)),
            dma((side, chunks - 1)),
            dma((side,)),
            dma((nx,)),
            dma((grid_count,)),
            dma,
            dma((11,)),
            dma,
            dma((groups, row_blocks)),
            dma((max(1, nx - 1),)),
            dma((groups, row_blocks, max(1, nx - 1))),
            dma,
            dma,
            dma,
            dma,
            dma,
            dma,
            dma,
            dma,
        ],
        compiler_params=pltpu.CompilerParams(
            collective_id=0, has_side_effects=True, vmem_limit_bytes=VMEM_LIMIT
        ),
    )(
        *[
            pltpu.with_memory_space_constraint(operand, pltpu.HBM)
            for operand in (
                sig_blocks,
                domain_blocks,
                point_values,
                density,
                coulomb_core,
                screen_mask,
                ao_centers,
                ao_widths.reshape(1, total),
                point_coords,
                lmo_coeffs,
            )
        ]
    )


def solution(mesh):
    in_specs = (
        P("grid", "tile"),
        P("grid", None),
        P("grid", "tile"),
        P(),
        P(),
        P(),
        P(),
        P(None, "grid"),
        P("tile", None),
        P(),
    )
    out_specs = P("tile", "grid")
    return jax.shard_map(shards, mesh=mesh, in_specs=in_specs, out_specs=out_specs, check_vma=False)
```

```python
import functools
import math

import jax
import jax.numpy as jnp
from jax import lax
from jax.experimental import pallas as pl
from jax.experimental.pallas import tpu as pltpu
from jax.sharding import PartitionSpec as P

MESH = pl.DeviceIdType.MESH
VMEM_LIMIT = 48 * 1024 * 1024
CHUNK = 512
FILL = 128
f32 = jnp.float32
bf16 = jnp.bfloat16
NT = (((1,), (1,)), ((), ()))
TN = (((0,), (0,)), ((), ()))


def grid_split(grid_count):
    inner = max(1, math.isqrt(max(1, grid_count // 2)))
    while grid_count % inner:
        inner -= 1
    return grid_count // inner, inner


def column_cuts(cols):
    early = max(128, cols * 4 // 32 // 128 * 128)
    cuts = [(start, min(CHUNK, cols - early - start)) for start in range(0, cols - early, CHUNK)]
    return cuts + [(cols - early, early)]


def remote(src, dst, send_sem, recv_sem, device):
    return pltpu.make_async_remote_copy(
        src_ref=src,
        dst_ref=dst,
        send_sem=send_sem,
        recv_sem=recv_sem,
        device_id=device,
        device_id_type=MESH,
    )


def listed(table_ref, row, block_id):
    flag = jnp.float32(0.0)
    for i in range(table_ref.shape[1]):
        flag = jnp.where(table_ref[row, i] == block_id, jnp.float32(1.0), flag)
    return flag


def dot(a, b, dims=(((1,), (0,)), ((), ()))):
    return lax.dot_general(a, b, dims, preferred_element_type=f32)


def kernel(
    nz,
    ny,
    nx,
    sig_hbm,
    domain_hbm,
    value_hbm,
    density_hbm,
    core_hbm,
    mask_hbm,
    centers_hbm,
    widths_hbm,
    coords_hbm,
    lmo_hbm,
    out_ref,
    sig_ref,
    domain_ref,
    value_ref,
    all_ref,
    stage_ref,
    turned_ref,
    acc_ref,
    part_ref,
    sibling_ref,
    pair_ref,
    peer_ref,
    total_ref,
    back_ref,
    core_ref,
    mask_ref,
    centers_ref,
    widths_ref,
    coords_ref,
    lmo_ref,
    scaled_ref,
    spread_ref,
    weighted_ref,
    pot_ref,
    got_ref,
    flat_ref,
    send_ref,
    share_ref,
    own_ref,
    weights_ref,
    rows_ref,
    flags_ref,
    product_ref,
    zs,
    zr,
    ds_,
    dr,
    ys,
    ye,
    yl,
    yt,
    es,
    er,
    local_sem,
    load_sem,
    cs,
    cr,
    xs,
    xr,
    gs,
    gr,
    vs,
    vr,
    ws,
    wr,
    fs,
    fr,
):
    grid_count, tile_count, nc = nz * ny, nx * 2, 2
    batch, cols = value_ref.shape
    rows = turned_ref.shape[1]
    block = core_ref.shape[0]
    blocks = mask_ref.shape[0]
    slab = batch // tile_count
    tile_blocks = cols // block
    row_blocks = rows // block
    cuts = column_cuts(cols)
    chunks = len(cuts)
    early = cuts[-1][1]
    tip = chunks - 1
    strips = domain_ref.shape[0]
    strip_width = lmo_ref.shape[1] // strips
    per_tile = strips // tile_count

    g, t = lax.axis_index("grid"), lax.axis_index("tile")
    z, y = g // ny, g % ny
    x, c = t // nc, t % nc
    place = c * nx + x
    has_left, has_right = z > 0, z < nz - 1
    left = (lax.rem(z + nz - 1, nz) * ny + y, t)
    right = (lax.rem(z + 1, nz) * ny + y, t)
    y_peers = [(z * ny + lax.rem(y + d, ny), t) for d in range(1, ny)]
    x_peers = [(g, lax.rem(x + d, nx) * nc + c) for d in range(1, nx)]
    sibling = (g, x * nc + (1 - c))
    far_tiles = [
        lax.rem(x + d, nx) * nc + (c if e == 0 else 1 - c) for d in range(1, nx) for e in range(nc)
    ]
    tile_order = far_tiles + [x * nc + (1 - c), t]

    small_loads = [
        pltpu.make_async_copy(src, dst, load_sem.at[i])
        for i, (src, dst) in enumerate(
            [
                (sig_hbm, sig_ref),
                (value_hbm, value_ref),
                (domain_hbm, domain_ref),
                (coords_hbm, coords_ref),
                (widths_hbm, widths_ref),
                (centers_hbm, centers_ref),
                (mask_hbm, mask_ref),
                (core_hbm, core_ref),
                (lmo_hbm, lmo_ref),
            ]
        )
    ]
    core_load, lmo_load = small_loads[7:]
    first_loads, small_loads = small_loads[:2], small_loads[2:7]

    def stage_load(i):
        return pltpu.make_async_copy(
            density_hbm.at[pl.ds(i * block, block)], stage_ref.at[i % 2], load_sem.at[9 + i % 2]
        )

    for load in first_loads + small_loads:
        load.start()
    for i in range(min(2, row_blocks)):
        stage_load(i).start()
    core_load.start()

    barrier = pltpu.get_barrier_semaphore()

    def hello(device):
        pl.semaphore_signal(barrier, inc=1, device_id=device, device_id_type=MESH)

    @pl.when(has_left)
    def _():
        hello(left)

    @pl.when(has_right)
    def _():
        hello(right)

    for peer in y_peers + [(g, tile) for tile in tile_order[:-1]]:
        hello(peer)

    for load in first_loads:
        load.wait()
    for m in range(tile_blocks):
        lanes = slice(m * block, (m + 1) * block)
        flag = listed(sig_ref, 0, t * tile_blocks + m)
        all_ref[g, :, lanes] = (value_ref[:, lanes].astype(f32) * flag).astype(bf16)

    neighbours = (
        ny - 1 + tile_count - 1 + jnp.where(has_left, 1, 0) + jnp.where(has_right, 1, 0)
    )
    pl.semaphore_wait(barrier, neighbours)

    def source(line, d):
        return line * ny + lax.rem(y + ny - d, ny)

    def piece(src, q):
        return all_ref.at[src, :, pl.ds(*cuts[q])]

    def z_sems(lane, line, d, q):
        slot = line - lane
        if d == 0:
            return zs.at[lane, line], zr.at[slot, q]
        return ds_.at[lane, line, d - 1], dr.at[slot, d - 1]

    def along(line, d, q, lane):
        spot = piece(source(line, d), q)
        send, recv = z_sems(lane, line, d, q)
        return remote(spot, spot, send, recv, left if lane else right)

    def across(line, d, q, sems):
        spot = piece(source(line, 0), q)
        return remote(spot, spot, *sems, y_peers[d - 1])

    def along_arrived(line, d, q, lane):
        spot = piece(source(line, d), q)
        send, recv = z_sems(lane, line, d, q)
        remote(spot, spot, send, recv, right).wait_recv()

    def arrived(spot, recv):
        remote(spot, spot, ys.at[0, 0], recv, right).wait_recv()

    def both_ways(d, q):
        @pl.when(has_right)
        def _():
            along(z, d, q, 0).start()

        @pl.when(has_left)
        def _():
            along(z, d, q, 1).start()

    half = nz // 2

    def send_across(i, line, q):
        if q != tip:
            for d in range(1, ny):
                recv = ye.at[d - 1, i] if i < nz - 1 else yl.at[d - 1, q]
                across(line, d, q, (ys.at[d - 1, i], recv)).start()

    for d in range(1, ny):
        across(z, d, tip, (ys.at[d - 1, nz], yt.at[d - 1])).start()
    for q in range(chunks):
        both_ways(0, q)
        send_across(0, z, q)
    def turn(i, k):
        if k == 0:
            stage_load(i).wait()
        lanes = slice(k * block, (k + 1) * block)
        turned_ref[lanes, i * block : (i + 1) * block] = stage_ref[i % 2, :, lanes].T
        if k == tile_blocks - 1:
            if i + 2 < row_blocks:
                stage_load(i + 2).start()
            if i == row_blocks - 1:
                lmo_load.start()

    turns = [functools.partial(turn, i, k) for i in range(row_blocks) for k in range(tile_blocks)]

    def pump(work, count=1):
        for _ in range(min(count, len(work))):
            work.pop(0)()

    for load in small_loads:
        load.wait()
    point = lax.broadcasted_iota(jnp.int32, (slab, batch), 1)
    wanted = lax.broadcasted_iota(jnp.int32, (slab, batch), 0) + place * slab
    here = [
        jnp.sum(
            jnp.where(point == wanted, coords_ref[d : d + 1, :], 0.0), axis=1, keepdims=True
        )
        for d in range(3)
    ]
    for j in range(blocks):
        lanes = slice(j * block, (j + 1) * block)
        distance = None
        for d in range(3):
            offset = centers_ref[d : d + 1, lanes] - here[d]
            distance = offset * offset if distance is None else distance + offset * offset
        coefficient = 1.0 / jnp.sqrt(distance + widths_ref[0:1, lanes])
        scaled_ref[j * slab : (j + 1) * slab, :] = coefficient * listed(sig_ref, 0, j)

    pump(turns, tile_blocks)
    for d in range(1, ny):
        arrived(piece(source(z, d), tip), yt.at[d - 1])
        both_ways(d, tip)

    total_rows = blocks * slab
    row = lax.broadcasted_iota(jnp.int32, (total_rows, blocks), 0)
    first = lax.broadcasted_iota(jnp.int32, (total_rows, blocks), 1) * slab
    expand = jnp.where((row >= first) & (row < first + slab), 1.0, 0.0).astype(bf16)
    screen = mask_ref[...].astype(f32).astype(bf16)
    spread = dot(dot(expand, screen).astype(bf16), expand, NT)
    row = lax.broadcasted_iota(jnp.int32, (total_rows, total_rows), 0)
    column = lax.broadcasted_iota(jnp.int32, (total_rows, total_rows), 1)
    spread_ref[...] = jnp.where(
        lax.rem(row, slab) == lax.rem(column, slab), spread, 0.0
    ).astype(bf16)
    for s in range(strips):
        for m in range(tile_blocks):
            flags_ref[s, m] = listed(domain_ref, s, t * tile_blocks + m)

    near = jnp.minimum(z, nz - 1 - z)

    def nearest(i):
        step = (i + 1) // 2 if i % 2 else -(i // 2)
        low = z < nz - 1 - z
        paired = jnp.where(low, z + step, z - step)
        single = jnp.where(low, i, nz - 1 - i)
        return jnp.where(i <= 2 * near, paired, single)

    order = [nearest(i) for i in range(nz)]
    inner = near > 0
    if nz > 2:
        order[-2:] = [
            jnp.where(inner, order[-1], order[-2]), jnp.where(inner, order[-2], order[-1])
        ]

    row_start = pl.multiple_of((g * rows) % cols, rows)
    owner = (g * rows) // cols
    is_owner = owner == t
    in_column = owner % nc == c

    def share(line, d):
        src = source(line, d)

        @pl.when(is_owner)
        def _():
            for i, peer in enumerate(x_peers + [sibling]):
                remote(
                    all_ref.at[src, :, pl.ds(row_start, rows)],
                    rows_ref.at[src],
                    es.at[i],
                    er.at[src],
                    peer,
                ).start()

    def take_across(i):
        for d in range(1, ny):
            arrived(all_ref.at[0, :, pl.ds(0, cols - early)], ye.at[d - 1, i])
            share(order[i], d)

    def serve(step, q, sources):
        for lane, line, here_, onward in (
            (0, z - step, z >= step, has_right),
            (1, z + step, z + step <= nz - 1, has_left),
        ):

            @pl.when(here_)
            def _():
                for d in sources:
                    along_arrived(line, d, q, lane)

                    @pl.when(onward)
                    def _():
                        along(line, d, q, lane).start()

    members = [source(order[i], d) for i in range(nz) for d in range(ny)]
    lines = [list(range(half))] + [[i] for i in range(half, nz)]
    spans = [(group[0] * ny, (group[-1] + 1) * ny) for group in lines]
    final = len(lines) - 1
    early_part = tip // 2 + 1
    sequence = [
        part
        for part in (
            list(range(min(early_part, tip - 1))),
            list(range(early_part, tip - 1)),
            [tip],
            [tip - 1],
        )
        if part
    ]

    def gathered(group, start, width):
        first, stop = spans[group]
        sources = members[first:stop]
        if group != final or width > 2 * CHUNK:
            sources = sources * max(1, FILL // ((stop - first) * batch))
        return jnp.concatenate(
            [all_ref[src, :, start : start + width] for src in sources], axis=0
        )

    def multiply(part):
        start = cuts[part[0]][0]
        width = sum(cuts[q][1] for q in part)
        for q in part:
            if q != tip:
                for d in range(1, ny):
                    arrived(piece(0, q), yl.at[d - 1, q])
        values = gathered(final, start, width)
        for i in range(row_blocks):
            lanes = slice(i * block, (i + 1) * block)
            value = dot(values, turned_ref[start : start + width, lanes])
            if part is not sequence[0]:
                value = acc_ref[:, lanes] + value[: acc_ref.shape[0]]
            if part is sequence[-1]:
                store_part(final, i, value)
            else:
                acc_ref[:, lanes] = value[: acc_ref.shape[0]]

    def store_part(group, i, value):
        first, stop = spans[group]
        size = stop - first
        value = value[: size * batch]
        if slab % 8 == 0:
            split = value.reshape(size, nc, nx, slab, block).astype(bf16)
            for e in range(nc):
                for h in range(nx):
                    part_ref[i, e, h, first:stop] = split[:, e, h]
        else:
            for n in range(size):
                for e in range(nc):
                    for h in range(nx):
                        row = ((n * nc + e) * nx + h) * slab
                        part_ref[i, e, h, first + n] = value[row : row + slab].astype(bf16)
        core_copy(group, i).start()

    def span_of(group):
        first, stop = spans[group]
        return pl.ds(first, stop - first)

    def core_copy(group, i):
        span = span_of(group)
        return remote(
            part_ref.at[i, 1 - c, :, span],
            sibling_ref.at[i, :, span],
            cs,
            cr.at[group, i],
            sibling,
        )

    def pair_copy(group, i, d):
        span = span_of(group)
        return remote(
            pair_ref.at[i, d - 1, span],
            peer_ref.at[i, d - 1, span],
            xs.at[d - 1],
            xr.at[group, i, d - 1],
            x_peers[d - 1],
        )

    def exchange(group, i):
        span = slice(*spans[group])
        core_copy(group, i).wait_recv()
        for d in range(1, nx):
            column = lax.rem(x + d, nx)
            pair_ref[i, d - 1, span] = (
                part_ref[i, c, column, span].astype(f32)
                + sibling_ref[i, column, span].astype(f32)
            ).astype(bf16)
            pair_copy(group, i, d).start()

    def collect(group, i):
        first, stop = spans[group]
        span = slice(first, stop)
        for d in range(1, nx):
            pair_copy(group, i, d).wait_recv()
        value = part_ref[i, c, x, span].astype(f32) + sibling_ref[i, x, span].astype(f32)
        for d in range(1, nx):
            value = value + peer_ref[i, d - 1, span].astype(f32)
        total_ref[i, span] = value.astype(bf16)
        for n in reversed(range(first, stop)):
            if n:
                remote(
                    total_ref.at[i, n], back_ref.at[g, i], gs, gr, (members[n], t)
                ).start()
            else:
                back_ref[g, i] = total_ref[i, n]

    def group_product(group, i):
        if i == 0:
            for line in lines[group]:
                if line:
                    take_across(line)
        store_part(
            group,
            i,
            dot(
                gathered(group, 0, cols), turned_ref[:, i * block : (i + 1) * block]
            ),
        )
        if i > 1:
            exchange(group, i - 2)

    items, after = [], []

    def enqueue(group):
        items.extend(functools.partial(group_product, group, i) for i in range(row_blocks))
        for i in range(max(0, row_blocks - 2), row_blocks):
            items.append(functools.partial(exchange, group, i))
        after.extend(functools.partial(collect, group, i) for i in range(row_blocks))

    share(z, 0)
    for step in range(1, nz):
        for q in range(chunks):
            serve(step, q, (0,))
            if step < nz - 1:
                send_across(step, order[step], q)
            else:
                if q == 0:

                    @pl.when(inner)
                    def _():
                        for ahead in range(tip):
                            send_across(step, order[step], ahead)

                @pl.when(jnp.logical_not(inner))
                def _():
                    send_across(step, order[step], q)

            pump(turns, 3)
            if (step, q) == (half, chunks // 2 + 1):
                pump(turns, len(turns))
                enqueue(0)
            if half < step and q == 2:
                enqueue(step - half)
            pump(items)
        serve(step, tip, range(1, ny))
        if step == 1:
            take_across(0)
        if step < nz - 1:
            share(order[step], 0)
    pump(items, len(items))
    for part in sequence:
        multiply(part)
        if part is not sequence[-1]:
            pump(after, 2)
    for i in range(row_blocks):
        exchange(final, i)
    pump(after, len(after))
    for i in range(row_blocks):
        collect(final, i)

    for d in range(ny):
        share(order[nz - 1], d)

    own_rows = pltpu.make_async_copy(
        all_ref.at[:, :, pl.ds(row_start, rows)], rows_ref, local_sem
    )

    @pl.when(is_owner)
    def _():
        own_rows.start()

    core_load.wait()
    def wait_all(spot, recv):
        remote(spot, spot, gs, recv, right).wait_recv()

    wait_all(back_ref.at[pl.ds(0, grid_count - 1)], gr)
    for j in range(blocks):
        span = slice(j * slab, (j + 1) * slab)
        weighted_ref[span, :] = scaled_ref[span, :] * back_ref[
            j // row_blocks, j % row_blocks
        ].astype(f32)
    weighted = weighted_ref[...].astype(bf16)

    tile_rows = tile_blocks * slab
    for n, tile in enumerate(tile_order):
        span = pl.ds(pl.multiple_of(tile * tile_rows, tile_rows), tile_rows)
        screened = dot(spread_ref[span, :], weighted).astype(bf16)
        potential = scaled_ref[span, :] * dot(screened, core_ref[...], NT)
        is_own = n == len(tile_order) - 1
        for m in range(tile_blocks):
            value = potential[m * slab : (m + 1) * slab, :].astype(bf16)
            if is_own:
                got_ref[place, m] = value
            else:
                pot_ref[n, m] = value
        if not is_own:
            remote(
                pot_ref.at[n], got_ref.at[place], vs, vr, (g, tile)
            ).start()

    lmo_load.wait()
    wait_all(got_ref.at[pl.ds(0, tile_count - 1)], vr)
    for i in range(tile_count):
        for m in range(tile_blocks):
            flat_ref[i * slab : (i + 1) * slab, m * block : (m + 1) * block] = got_ref[
                i, m
            ].astype(f32)

    own_total = None
    group_width = nc * per_tile * strip_width
    for n, (d, tiles) in enumerate(
        [(d, tile_order[2 * d - 2 : 2 * d]) for d in range(1, nx)] + [(0, tile_order[-2:])]
    ):
        plane = lax.rem(x + d, nx)
        kept = jnp.concatenate(
            [
                jnp.concatenate(
                    [
                        (
                            flat_ref[:, m * block : (m + 1) * block]
                            * flags_ref[plane * nc * per_tile + k, m]
                        ).astype(bf16)
                        for m in range(tile_blocks)
                    ],
                    axis=1,
                )
                for k in range(nc * per_tile)
            ],
            axis=0,
        )
        start = pl.multiple_of(plane * group_width, group_width)
        copies = max(1, FILL // kept.shape[0])
        values = dot(
            jnp.concatenate([kept] * copies, axis=0), lmo_ref[:, pl.ds(start, group_width)]
        )
        pieces = []
        for e in range(nc):
            parts = []
            for k in range(e * per_tile, (e + 1) * per_tile):
                parts.append(
                    values[
                        k * batch : (k + 1) * batch, k * strip_width : (k + 1) * strip_width
                    ]
                )
            pieces.append(parts[0] if per_tile == 1 else jnp.concatenate(parts, axis=1))
        for e in range(nc):
            product_ref[n, e] = pieces[e]
        for k, tile in enumerate(tiles):
            index = n * nc + k
            chosen = product_ref[n, lax.rem(tile, nc)]
            if index < tile_count - 1:
                send_ref[index] = chosen.astype(bf16)
                remote(send_ref.at[index], share_ref.at[t], ws, wr, (g, tile)).start()
            else:
                own_total = chosen
    wait_all(share_ref.at[pl.ds(0, tile_count - 1)], wr)
    for tile in tile_order[:-1]:
        own_total = own_total + share_ref[tile].astype(f32)
    own_ref[...] = own_total.astype(bf16)
    for target in reversed(members[1:]):
        remote(own_ref, weights_ref.at[g], fs, fr, (target, t)).start()
    weights_ref[g] = own_ref[...]

    @pl.when(jnp.logical_and(in_column, jnp.logical_not(is_owner)))
    def _():
        for src in range(grid_count):
            spot = rows_ref.at[src]
            pass_on = remote(spot, spot, es.at[nx - 1], er.at[src], sibling)
            pass_on.wait_recv()
            pass_on.start()

    @pl.when(is_owner)
    def _():
        own_rows.wait()

    @pl.when(jnp.logical_not(in_column))
    def _():
        for src in range(grid_count):
            spot = rows_ref.at[src]
            remote(spot, spot, es.at[0], er.at[src], right).wait_recv()

    wait_all(weights_ref.at[pl.ds(0, grid_count - 1)], fr)
    out_ref[...] = dot(
        weights_ref[...].reshape(grid_count * batch, weights_ref.shape[2]),
        rows_ref[...].reshape(grid_count * batch, rows),
        TN,
    ).astype(bf16)

    def drain(ref, sem):
        remote(ref, ref, sem, fr, right).wait_send()

    for line in range(nz):
        for lane, sent in (
            (0, jnp.logical_and(has_right, line <= z)),
            (1, jnp.logical_and(has_left, line >= z)),
        ):

            @pl.when(sent)
            def _():
                drain(all_ref.at[0], zs.at[lane, line])
                for d in range(1, ny):
                    drain(all_ref.at[0, :, pl.ds(cols - early, early)], ds_.at[lane, line, d - 1])

    for d in range(1, ny):
        for i in range(nz):
            drain(all_ref.at[0, :, pl.ds(0, cols - early)], ys.at[d - 1, i])
        drain(all_ref.at[0, :, pl.ds(0, early)], ys.at[d - 1, nz])

    @pl.when(is_owner)
    def _():
        for i in range(nx):
            drain(rows_ref, es.at[i])

    @pl.when(jnp.logical_and(in_column, jnp.logical_not(is_owner)))
    def _():
        drain(rows_ref, es.at[nx - 1])

    drain(sibling_ref, cs)
    for d in range(1, nx):
        drain(pair_ref.at[:, d - 1], xs.at[d - 1])
    drain(back_ref.at[pl.ds(0, grid_count - 1)], gs)
    drain(pot_ref, vs)
    drain(send_ref, ws)
    drain(weights_ref.at[pl.ds(0, grid_count - 1)], fs)


def shards(
    point_values,
    sig_blocks,
    density,
    coulomb_core,
    screen_mask,
    ao_centers,
    ao_widths,
    point_coords,
    lmo_coeffs,
    domain_blocks,
):
    grid_count, tile_count = lax.axis_size("grid"), lax.axis_size("tile")
    nz, ny = grid_split(grid_count)
    nc, nx = 2, tile_count // 2
    rows, cols = density.shape
    batch = point_values.shape[0]
    block = coulomb_core.shape[0]
    total = ao_widths.shape[0]
    blocks = total // block
    slab = batch // tile_count
    strip = lmo_coeffs.shape[1] // tile_count
    tile_blocks, row_blocks, chunks = cols // block, rows // block, len(column_cuts(cols))
    dma = pltpu.SemaphoreType.DMA
    vmem = pl.BlockSpec(memory_space=pltpu.VMEM)
    anywhere = pl.BlockSpec(memory_space=pltpu.HBM)
    side = max(1, ny - 1)
    groups = 1 + nz - nz // 2
    return pl.pallas_call(
        functools.partial(kernel, nz, ny, nx),
        out_shape=jax.ShapeDtypeStruct((strip, rows), bf16),
        in_specs=[anywhere] * 10,
        out_specs=vmem,
        scratch_shapes=[
            pltpu.SMEM(sig_blocks.shape, jnp.int32),
            pltpu.SMEM(domain_blocks.shape, jnp.int32),
            pltpu.VMEM((batch, cols), bf16),
            pltpu.VMEM((grid_count, batch, cols), bf16),
            pltpu.VMEM((2, block, cols), bf16),
            pltpu.VMEM((cols, rows), bf16),
            pltpu.VMEM((ny * batch, rows), f32),
            pltpu.VMEM((row_blocks, nc, nx, grid_count, slab, block), bf16),
            pltpu.VMEM((row_blocks, nx, grid_count, slab, block), bf16),
            pltpu.VMEM((row_blocks, max(1, nx - 1), grid_count, slab, block), bf16),
            pltpu.VMEM((row_blocks, max(1, nx - 1), grid_count, slab, block), bf16),
            pltpu.VMEM((row_blocks, grid_count, slab, block), bf16),
            pltpu.VMEM((grid_count, row_blocks, slab, block), bf16),
            pltpu.VMEM(coulomb_core.shape, bf16),
            pltpu.VMEM(screen_mask.shape, jnp.int32),
            pltpu.VMEM(ao_centers.shape, f32),
            pltpu.VMEM((1, total), f32),
            pltpu.VMEM(point_coords.shape, f32),
            pltpu.VMEM(lmo_coeffs.shape, bf16),
            pltpu.VMEM((blocks * slab, block), f32),
            pltpu.VMEM((blocks * slab, blocks * slab), bf16),
            pltpu.VMEM((blocks * slab, block), f32),
            pltpu.VMEM((tile_count - 1, tile_blocks, slab, block), bf16),
            pltpu.VMEM((tile_count, tile_blocks, slab, block), bf16),
            pltpu.VMEM((batch, cols), f32),
            pltpu.VMEM((tile_count - 1, batch, strip), bf16),
            pltpu.VMEM((tile_count, batch, strip), bf16),
            pltpu.VMEM((batch, strip), bf16),
            pltpu.VMEM((grid_count, batch, strip), bf16),
            pltpu.VMEM((grid_count, batch, rows), bf16),
            pltpu.SMEM((domain_blocks.shape[0], tile_blocks), f32),
            pltpu.VMEM((nx, nc, batch, strip), f32),
            dma((2, nz)),
            dma((nz - 1, chunks)),
            dma((2, nz, side)),
            dma((nz - 1, side)),
            dma((side, nz + 1)),
            dma((side, nz - 1)),
            dma((side, chunks - 1)),
            dma((side,)),
            dma((nx,)),
            dma((grid_count,)),
            dma,
            dma((11,)),
            dma,
            dma((groups, row_blocks)),
            dma((max(1, nx - 1),)),
            dma((groups, row_blocks, max(1, nx - 1))),
            dma,
            dma,
            dma,
            dma,
            dma,
            dma,
            dma,
            dma,
        ],
        compiler_params=pltpu.CompilerParams(
            collective_id=0, has_side_effects=True, vmem_limit_bytes=VMEM_LIMIT
        ),
    )(
        *[
            pltpu.with_memory_space_constraint(operand, pltpu.HBM)
            for operand in (
                sig_blocks,
                domain_blocks,
                point_values,
                density,
                coulomb_core,
                screen_mask,
                ao_centers,
                ao_widths.reshape(1, total),
                point_coords,
                lmo_coeffs,
            )
        ]
    )


def solution(mesh):
    in_specs = (
        P("grid", "tile"),
        P("grid", None),
        P("grid", "tile"),
        P(),
        P(),
        P(),
        P(),
        P(None, "grid"),
        P("tile", None),
        P(),
    )
    out_specs = P("tile", "grid")
    return jax.shard_map(shards, mesh=mesh, in_specs=in_specs, out_specs=out_specs, check_vma=False)
```

```python
import functools
import math

import jax
import jax.numpy as jnp
from jax import lax
from jax.experimental import pallas as pl
from jax.experimental.pallas import tpu as pltpu
from jax.sharding import PartitionSpec as P

MESH = pl.DeviceIdType.MESH
VMEM_LIMIT = 48 * 1024 * 1024
CHUNK = 512
FILL = 128
f32 = jnp.float32
bf16 = jnp.bfloat16
NT = (((1,), (1,)), ((), ()))
TN = (((0,), (0,)), ((), ()))


def grid_split(grid_count):
    inner = max(1, math.isqrt(max(1, grid_count // 2)))
    while grid_count % inner:
        inner -= 1
    return grid_count // inner, inner


def column_cuts(cols):
    early = max(128, cols * 4 // 32 // 128 * 128)
    cuts = [(start, min(CHUNK, cols - early - start)) for start in range(0, cols - early, CHUNK)]
    return cuts + [(cols - early, early)]


def remote(src, dst, send_sem, recv_sem, device):
    return pltpu.make_async_remote_copy(
        src_ref=src,
        dst_ref=dst,
        send_sem=send_sem,
        recv_sem=recv_sem,
        device_id=device,
        device_id_type=MESH,
    )


def listed(table_ref, row, block_id):
    flag = jnp.float32(0.0)
    for i in range(table_ref.shape[1]):
        flag = jnp.where(table_ref[row, i] == block_id, jnp.float32(1.0), flag)
    return flag


def dot(a, b, dims=(((1,), (0,)), ((), ()))):
    return lax.dot_general(a, b, dims, preferred_element_type=f32)


def kernel(
    nz,
    ny,
    nx,
    sig_hbm,
    domain_hbm,
    value_hbm,
    density_hbm,
    core_hbm,
    mask_hbm,
    centers_hbm,
    widths_hbm,
    coords_hbm,
    lmo_hbm,
    out_ref,
    sig_ref,
    domain_ref,
    value_ref,
    all_ref,
    stage_ref,
    turned_ref,
    acc_ref,
    part_ref,
    sibling_ref,
    pair_ref,
    peer_ref,
    total_ref,
    back_ref,
    core_ref,
    mix_ref,
    mask_ref,
    centers_ref,
    widths_ref,
    coords_ref,
    lmo_ref,
    scaled_ref,
    spread_ref,
    weighted_ref,
    pot_ref,
    got_ref,
    flat_ref,
    send_ref,
    share_ref,
    own_ref,
    weights_ref,
    rows_ref,
    flags_ref,
    product_ref,
    zs,
    zr,
    ds_,
    dr,
    ys,
    ye,
    yl,
    yt,
    es,
    er,
    local_sem,
    load_sem,
    cs,
    cr,
    xs,
    xr,
    gs,
    gr,
    vs,
    vr,
    ws,
    wr,
    fs,
    fr,
):
    grid_count, tile_count, nc = nz * ny, nx * 2, 2
    batch, cols = value_ref.shape
    rows = turned_ref.shape[1]
    block = core_ref.shape[0]
    blocks = mask_ref.shape[0]
    slab = batch // tile_count
    tile_blocks = cols // block
    row_blocks = rows // block
    cuts = column_cuts(cols)
    chunks = len(cuts)
    early = cuts[-1][1]
    tip = chunks - 1
    strips = domain_ref.shape[0]
    strip_width = lmo_ref.shape[1] // strips
    per_tile = strips // tile_count

    g, t = lax.axis_index("grid"), lax.axis_index("tile")
    z, y = g // ny, g % ny
    x, c = t // nc, t % nc
    place = c * nx + x
    has_left, has_right = z > 0, z < nz - 1
    left = (lax.rem(z + nz - 1, nz) * ny + y, t)
    right = (lax.rem(z + 1, nz) * ny + y, t)
    y_peers = [(z * ny + lax.rem(y + d, ny), t) for d in range(1, ny)]
    x_peers = [(g, lax.rem(x + d, nx) * nc + c) for d in range(1, nx)]
    sibling = (g, x * nc + (1 - c))
    far_tiles = [
        lax.rem(x + d, nx) * nc + (c if e == 0 else 1 - c) for d in range(1, nx) for e in range(nc)
    ]
    tile_order = far_tiles + [x * nc + (1 - c), t]

    small_loads = [
        pltpu.make_async_copy(src, dst, load_sem.at[i])
        for i, (src, dst) in enumerate(
            [
                (sig_hbm, sig_ref),
                (value_hbm, value_ref),
                (domain_hbm, domain_ref),
                (coords_hbm, coords_ref),
                (widths_hbm, widths_ref),
                (centers_hbm, centers_ref),
                (mask_hbm, mask_ref),
                (core_hbm, core_ref),
                (lmo_hbm, lmo_ref),
            ]
        )
    ]
    core_load, lmo_load = small_loads[7:]
    first_loads, small_loads = small_loads[:2], small_loads[2:7]

    def stage_load(i):
        return pltpu.make_async_copy(
            density_hbm.at[pl.ds(i * block, block)], stage_ref.at[i % 2], load_sem.at[9 + i % 2]
        )

    for load in first_loads + small_loads:
        load.start()
    for i in range(min(2, row_blocks)):
        stage_load(i).start()
    core_load.start()

    barrier = pltpu.get_barrier_semaphore()

    def hello(device):
        pl.semaphore_signal(barrier, inc=1, device_id=device, device_id_type=MESH)

    @pl.when(has_left)
    def _():
        hello(left)

    @pl.when(has_right)
    def _():
        hello(right)

    for peer in y_peers + [(g, tile) for tile in tile_order[:-1]]:
        hello(peer)

    for load in first_loads:
        load.wait()
    for m in range(tile_blocks):
        lanes = slice(m * block, (m + 1) * block)
        flag = listed(sig_ref, 0, t * tile_blocks + m)
        all_ref[g, :, lanes] = (value_ref[:, lanes].astype(f32) * flag).astype(bf16)

    neighbours = (
        ny - 1 + tile_count - 1 + jnp.where(has_left, 1, 0) + jnp.where(has_right, 1, 0)
    )
    pl.semaphore_wait(barrier, neighbours)

    def source(line, d):
        return line * ny + lax.rem(y + ny - d, ny)

    def piece(src, q):
        return all_ref.at[src, :, pl.ds(*cuts[q])]

    def z_sems(lane, line, d, q):
        slot = line - lane
        if d == 0:
            return zs.at[lane, line], zr.at[slot, q]
        return ds_.at[lane, line, d - 1], dr.at[slot, d - 1]

    def along(line, d, q, lane):
        spot = piece(source(line, d), q)
        send, recv = z_sems(lane, line, d, q)
        return remote(spot, spot, send, recv, left if lane else right)

    def across(line, d, q, sems):
        spot = piece(source(line, 0), q)
        return remote(spot, spot, *sems, y_peers[d - 1])

    def along_arrived(line, d, q, lane):
        spot = piece(source(line, d), q)
        send, recv = z_sems(lane, line, d, q)
        remote(spot, spot, send, recv, right).wait_recv()

    def arrived(spot, recv):
        remote(spot, spot, ys.at[0, 0], recv, right).wait_recv()

    def both_ways(d, q):
        @pl.when(has_right)
        def _():
            along(z, d, q, 0).start()

        @pl.when(has_left)
        def _():
            along(z, d, q, 1).start()

    half = nz // 2

    def send_across(i, line, q):
        if q != tip:
            for d in range(1, ny):
                recv = ye.at[d - 1, i] if i < nz - 1 else yl.at[d - 1, q]
                across(line, d, q, (ys.at[d - 1, i], recv)).start()

    for d in range(1, ny):
        across(z, d, tip, (ys.at[d - 1, nz], yt.at[d - 1])).start()
    for q in range(chunks):
        both_ways(0, q)
        send_across(0, z, q)
    def turn(i, k):
        if k == 0:
            stage_load(i).wait()
        lanes = slice(k * block, (k + 1) * block)
        turned_ref[lanes, i * block : (i + 1) * block] = stage_ref[i % 2, :, lanes].T
        if k == tile_blocks - 1:
            if i + 2 < row_blocks:
                stage_load(i + 2).start()
            if i == row_blocks - 1:
                lmo_load.start()

    def turn_core():
        core_load.wait()
        mix_ref[...] = core_ref[...].T

    turns = [functools.partial(turn, i, k) for i in range(row_blocks) for k in range(tile_blocks)]
    turns.append(turn_core)

    def pump(work, count=1):
        for _ in range(min(count, len(work))):
            work.pop(0)()

    for load in small_loads:
        load.wait()
    point = lax.broadcasted_iota(jnp.int32, (slab, batch), 1)
    wanted = lax.broadcasted_iota(jnp.int32, (slab, batch), 0) + place * slab
    here = [
        jnp.sum(
            jnp.where(point == wanted, coords_ref[d : d + 1, :], 0.0), axis=1, keepdims=True
        )
        for d in range(3)
    ]
    for j in range(blocks):
        lanes = slice(j * block, (j + 1) * block)
        distance = None
        for d in range(3):
            offset = centers_ref[d : d + 1, lanes] - here[d]
            distance = offset * offset if distance is None else distance + offset * offset
        coefficient = 1.0 / jnp.sqrt(distance + widths_ref[0:1, lanes])
        scaled_ref[j * slab : (j + 1) * slab, :] = coefficient * listed(sig_ref, 0, j)

    pump(turns, tile_blocks)
    for d in range(1, ny):
        arrived(piece(source(z, d), tip), yt.at[d - 1])
        both_ways(d, tip)

    total_rows = blocks * slab
    row = lax.broadcasted_iota(jnp.int32, (total_rows, blocks), 0)
    first = lax.broadcasted_iota(jnp.int32, (total_rows, blocks), 1) * slab
    expand = jnp.where((row >= first) & (row < first + slab), 1.0, 0.0).astype(bf16)
    screen = mask_ref[...].astype(f32).astype(bf16)
    spread = dot(dot(expand, screen).astype(bf16), expand, NT)
    row = lax.broadcasted_iota(jnp.int32, (total_rows, total_rows), 0)
    column = lax.broadcasted_iota(jnp.int32, (total_rows, total_rows), 1)
    spread_ref[...] = jnp.where(
        lax.rem(row, slab) == lax.rem(column, slab), spread, 0.0
    ).astype(bf16)
    for s in range(strips):
        for m in range(tile_blocks):
            flags_ref[s, m] = listed(domain_ref, s, t * tile_blocks + m)

    near = jnp.minimum(z, nz - 1 - z)

    def nearest(i):
        step = (i + 1) // 2 if i % 2 else -(i // 2)
        low = z < nz - 1 - z
        paired = jnp.where(low, z + step, z - step)
        single = jnp.where(low, i, nz - 1 - i)
        return jnp.where(i <= 2 * near, paired, single)

    order = [nearest(i) for i in range(nz)]
    inner = near > 0
    if nz > 2:
        order[-2:] = [
            jnp.where(inner, order[-1], order[-2]), jnp.where(inner, order[-2], order[-1])
        ]

    row_start = pl.multiple_of((g * rows) % cols, rows)
    owner = (g * rows) // cols
    is_owner = owner == t
    in_column = owner % nc == c

    def share(line, d):
        src = source(line, d)

        @pl.when(is_owner)
        def _():
            for i, peer in enumerate(x_peers + [sibling]):
                remote(
                    all_ref.at[src, :, pl.ds(row_start, rows)],
                    rows_ref.at[src],
                    es.at[i],
                    er.at[src],
                    peer,
                ).start()

    def take_across(i):
        for d in range(1, ny):
            arrived(all_ref.at[0, :, pl.ds(0, cols - early)], ye.at[d - 1, i])
            share(order[i], d)

    def serve(step, q, sources):
        for lane, line, here_, onward in (
            (0, z - step, z >= step, has_right),
            (1, z + step, z + step <= nz - 1, has_left),
        ):

            @pl.when(here_)
            def _():
                for d in sources:
                    along_arrived(line, d, q, lane)

                    @pl.when(onward)
                    def _():
                        along(line, d, q, lane).start()

    members = [source(order[i], d) for i in range(nz) for d in range(ny)]
    lines = [list(range(half))] + [[i] for i in range(half, nz)]
    spans = [(group[0] * ny, (group[-1] + 1) * ny) for group in lines]
    final = len(lines) - 1
    early_part = tip // 2 + 1
    sequence = [
        part
        for part in (
            list(range(min(early_part, tip - 1))),
            list(range(early_part, tip - 1)),
            [tip],
            [tip - 1],
        )
        if part
    ]

    def gathered(group, start, width):
        first, stop = spans[group]
        sources = members[first:stop]
        if group != final or width > 2 * CHUNK:
            sources = sources * max(1, FILL // ((stop - first) * batch))
        return jnp.concatenate(
            [all_ref[src, :, start : start + width] for src in sources], axis=0
        )

    def multiply(part):
        start = cuts[part[0]][0]
        width = sum(cuts[q][1] for q in part)
        for q in part:
            if q != tip:
                for d in range(1, ny):
                    arrived(piece(0, q), yl.at[d - 1, q])
        values = gathered(final, start, width)
        for i in range(row_blocks):
            lanes = slice(i * block, (i + 1) * block)
            value = dot(values, turned_ref[start : start + width, lanes])
            if part is not sequence[0]:
                value = acc_ref[:, lanes] + value[: acc_ref.shape[0]]
            if part is sequence[-1]:
                store_part(final, i, value)
            else:
                acc_ref[:, lanes] = value[: acc_ref.shape[0]]

    def store_part(group, i, value):
        first, stop = spans[group]
        size = stop - first
        value = value[: size * batch]
        if slab % 8 == 0:
            split = value.reshape(size, nc, nx, slab, block).astype(bf16)
            for e in range(nc):
                for h in range(nx):
                    part_ref[i, e, h, first:stop] = split[:, e, h]
        else:
            for n in range(size):
                for e in range(nc):
                    for h in range(nx):
                        row = ((n * nc + e) * nx + h) * slab
                        part_ref[i, e, h, first + n] = value[row : row + slab].astype(bf16)
        core_copy(group, i).start()

    def span_of(group):
        first, stop = spans[group]
        return pl.ds(first, stop - first)

    def core_copy(group, i):
        span = span_of(group)
        return remote(
            part_ref.at[i, 1 - c, :, span],
            sibling_ref.at[i, :, span],
            cs,
            cr.at[group, i],
            sibling,
        )

    def pair_copy(group, i, d):
        span = span_of(group)
        return remote(
            pair_ref.at[i, d - 1, span],
            peer_ref.at[i, d - 1, span],
            xs.at[d - 1],
            xr.at[group, i, d - 1],
            x_peers[d - 1],
        )

    def exchange(group, i):
        span = slice(*spans[group])
        core_copy(group, i).wait_recv()
        for d in range(1, nx):
            column = lax.rem(x + d, nx)
            pair_ref[i, d - 1, span] = (
                part_ref[i, c, column, span].astype(f32)
                + sibling_ref[i, column, span].astype(f32)
            ).astype(bf16)
            pair_copy(group, i, d).start()

    def collect(group, i):
        first, stop = spans[group]
        span = slice(first, stop)
        for d in range(1, nx):
            pair_copy(group, i, d).wait_recv()
        value = part_ref[i, c, x, span].astype(f32) + sibling_ref[i, x, span].astype(f32)
        for d in range(1, nx):
            value = value + peer_ref[i, d - 1, span].astype(f32)
        total_ref[i, span] = value.astype(bf16)
        for n in reversed(range(first, stop)):
            if n:
                remote(
                    total_ref.at[i, n], back_ref.at[g, i], gs, gr, (members[n], t)
                ).start()
            else:
                back_ref[g, i] = total_ref[i, n]

    def group_product(group, i):
        if i == 0:
            for line in lines[group]:
                if line:
                    take_across(line)
        store_part(
            group,
            i,
            dot(
                gathered(group, 0, cols), turned_ref[:, i * block : (i + 1) * block]
            ),
        )
        if i > 1:
            exchange(group, i - 2)

    items, after = [], []

    def enqueue(group):
        items.extend(functools.partial(group_product, group, i) for i in range(row_blocks))
        for i in range(max(0, row_blocks - 2), row_blocks):
            items.append(functools.partial(exchange, group, i))
        after.extend(functools.partial(collect, group, i) for i in range(row_blocks))

    share(z, 0)
    for step in range(1, nz):
        for q in range(chunks):
            serve(step, q, (0,))
            if step < nz - 1:
                send_across(step, order[step], q)
            else:
                if q == 0:

                    @pl.when(inner)
                    def _():
                        for ahead in range(tip):
                            send_across(step, order[step], ahead)

                @pl.when(jnp.logical_not(inner))
                def _():
                    send_across(step, order[step], q)

            pump(turns, 3)
            if (step, q) == (half, chunks // 2 + 1):
                pump(turns, len(turns))
                enqueue(0)
            if half < step and q == 2:
                enqueue(step - half)
            pump(items)
        serve(step, tip, range(1, ny))
        if step == 1:
            take_across(0)
        if step < nz - 1:
            share(order[step], 0)
    pump(items, len(items))
    for part in sequence:
        multiply(part)
        if part is not sequence[-1]:
            pump(after, 2)
    for i in range(row_blocks):
        exchange(final, i)
    pump(after, len(after))
    for i in range(row_blocks):
        collect(final, i)

    for d in range(ny):
        share(order[nz - 1], d)

    own_rows = pltpu.make_async_copy(
        all_ref.at[:, :, pl.ds(row_start, rows)], rows_ref, local_sem
    )

    @pl.when(is_owner)
    def _():
        own_rows.start()

    def wait_all(spot, recv):
        remote(spot, spot, gs, recv, right).wait_recv()

    wait_all(back_ref.at[pl.ds(0, grid_count - 1)], gr)
    for j in range(blocks):
        span = slice(j * slab, (j + 1) * slab)
        weighted_ref[span, :] = scaled_ref[span, :] * back_ref[
            j // row_blocks, j % row_blocks
        ].astype(f32)
    weighted = weighted_ref[...].astype(bf16)

    tile_rows = tile_blocks * slab
    for n, tile in enumerate(tile_order):
        span = pl.ds(pl.multiple_of(tile * tile_rows, tile_rows), tile_rows)
        screened = dot(spread_ref[span, :], weighted).astype(bf16)
        potential = scaled_ref[span, :] * dot(screened, mix_ref[...])
        is_own = n == len(tile_order) - 1
        for m in range(tile_blocks):
            value = potential[m * slab : (m + 1) * slab, :].astype(bf16)
            if is_own:
                got_ref[place, m] = value
            else:
                pot_ref[n, m] = value
        if not is_own:
            remote(
                pot_ref.at[n], got_ref.at[place], vs, vr, (g, tile)
            ).start()

    lmo_load.wait()
    wait_all(got_ref.at[pl.ds(0, tile_count - 1)], vr)
    for i in range(tile_count):
        for m in range(tile_blocks):
            flat_ref[i * slab : (i + 1) * slab, m * block : (m + 1) * block] = got_ref[
                i, m
            ].astype(f32)

    own_total = None
    group_width = nc * per_tile * strip_width
    for n, (d, tiles) in enumerate(
        [(d, tile_order[2 * d - 2 : 2 * d]) for d in range(1, nx)] + [(0, tile_order[-2:])]
    ):
        plane = lax.rem(x + d, nx)
        kept = jnp.concatenate(
            [
                jnp.concatenate(
                    [
                        (
                            flat_ref[:, m * block : (m + 1) * block]
                            * flags_ref[plane * nc * per_tile + k, m]
                        ).astype(bf16)
                        for m in range(tile_blocks)
                    ],
                    axis=1,
                )
                for k in range(nc * per_tile)
            ],
            axis=0,
        )
        start = pl.multiple_of(plane * group_width, group_width)
        copies = max(1, FILL // kept.shape[0])
        values = dot(
            jnp.concatenate([kept] * copies, axis=0), lmo_ref[:, pl.ds(start, group_width)]
        )
        pieces = []
        for e in range(nc):
            parts = []
            for k in range(e * per_tile, (e + 1) * per_tile):
                parts.append(
                    values[
                        k * batch : (k + 1) * batch, k * strip_width : (k + 1) * strip_width
                    ]
                )
            pieces.append(parts[0] if per_tile == 1 else jnp.concatenate(parts, axis=1))
        for e in range(nc):
            product_ref[n, e] = pieces[e]
        for k, tile in enumerate(tiles):
            index = n * nc + k
            chosen = product_ref[n, lax.rem(tile, nc)]
            if index < tile_count - 1:
                send_ref[index] = chosen.astype(bf16)
                remote(send_ref.at[index], share_ref.at[t], ws, wr, (g, tile)).start()
            else:
                own_total = chosen
    wait_all(share_ref.at[pl.ds(0, tile_count - 1)], wr)
    for tile in tile_order[:-1]:
        own_total = own_total + share_ref[tile].astype(f32)
    own_ref[...] = own_total.astype(bf16)
    for target in reversed(members[1:]):
        remote(own_ref, weights_ref.at[g], fs, fr, (target, t)).start()
    weights_ref[g] = own_ref[...]

    @pl.when(jnp.logical_and(in_column, jnp.logical_not(is_owner)))
    def _():
        for src in range(grid_count):
            spot = rows_ref.at[src]
            pass_on = remote(spot, spot, es.at[nx - 1], er.at[src], sibling)
            pass_on.wait_recv()
            pass_on.start()

    @pl.when(is_owner)
    def _():
        own_rows.wait()

    @pl.when(jnp.logical_not(in_column))
    def _():
        for src in range(grid_count):
            spot = rows_ref.at[src]
            remote(spot, spot, es.at[0], er.at[src], right).wait_recv()

    wait_all(weights_ref.at[pl.ds(0, grid_count - 1)], fr)
    out_ref[...] = dot(
        weights_ref[...].reshape(grid_count * batch, weights_ref.shape[2]),
        rows_ref[...].reshape(grid_count * batch, rows),
        TN,
    ).astype(bf16)

    def drain(ref, sem):
        remote(ref, ref, sem, fr, right).wait_send()

    for line in range(nz):
        for lane, sent in (
            (0, jnp.logical_and(has_right, line <= z)),
            (1, jnp.logical_and(has_left, line >= z)),
        ):

            @pl.when(sent)
            def _():
                drain(all_ref.at[0], zs.at[lane, line])
                for d in range(1, ny):
                    drain(all_ref.at[0, :, pl.ds(cols - early, early)], ds_.at[lane, line, d - 1])

    for d in range(1, ny):
        for i in range(nz):
            drain(all_ref.at[0, :, pl.ds(0, cols - early)], ys.at[d - 1, i])
        drain(all_ref.at[0, :, pl.ds(0, early)], ys.at[d - 1, nz])

    @pl.when(is_owner)
    def _():
        for i in range(nx):
            drain(rows_ref, es.at[i])

    @pl.when(jnp.logical_and(in_column, jnp.logical_not(is_owner)))
    def _():
        drain(rows_ref, es.at[nx - 1])

    drain(sibling_ref, cs)
    for d in range(1, nx):
        drain(pair_ref.at[:, d - 1], xs.at[d - 1])
    drain(back_ref.at[pl.ds(0, grid_count - 1)], gs)
    drain(pot_ref, vs)
    drain(send_ref, ws)
    drain(weights_ref.at[pl.ds(0, grid_count - 1)], fs)


def shards(
    point_values,
    sig_blocks,
    density,
    coulomb_core,
    screen_mask,
    ao_centers,
    ao_widths,
    point_coords,
    lmo_coeffs,
    domain_blocks,
):
    grid_count, tile_count = lax.axis_size("grid"), lax.axis_size("tile")
    nz, ny = grid_split(grid_count)
    nc, nx = 2, tile_count // 2
    rows, cols = density.shape
    batch = point_values.shape[0]
    block = coulomb_core.shape[0]
    total = ao_widths.shape[0]
    blocks = total // block
    slab = batch // tile_count
    strip = lmo_coeffs.shape[1] // tile_count
    tile_blocks, row_blocks, chunks = cols // block, rows // block, len(column_cuts(cols))
    dma = pltpu.SemaphoreType.DMA
    vmem = pl.BlockSpec(memory_space=pltpu.VMEM)
    anywhere = pl.BlockSpec(memory_space=pltpu.HBM)
    side = max(1, ny - 1)
    groups = 1 + nz - nz // 2
    return pl.pallas_call(
        functools.partial(kernel, nz, ny, nx),
        out_shape=jax.ShapeDtypeStruct((strip, rows), bf16),
        in_specs=[anywhere] * 10,
        out_specs=vmem,
        scratch_shapes=[
            pltpu.SMEM(sig_blocks.shape, jnp.int32),
            pltpu.SMEM(domain_blocks.shape, jnp.int32),
            pltpu.VMEM((batch, cols), bf16),
            pltpu.VMEM((grid_count, batch, cols), bf16),
            pltpu.VMEM((2, block, cols), bf16),
            pltpu.VMEM((cols, rows), bf16),
            pltpu.VMEM((ny * batch, rows), f32),
            pltpu.VMEM((row_blocks, nc, nx, grid_count, slab, block), bf16),
            pltpu.VMEM((row_blocks, nx, grid_count, slab, block), bf16),
            pltpu.VMEM((row_blocks, max(1, nx - 1), grid_count, slab, block), bf16),
            pltpu.VMEM((row_blocks, max(1, nx - 1), grid_count, slab, block), bf16),
            pltpu.VMEM((row_blocks, grid_count, slab, block), bf16),
            pltpu.VMEM((grid_count, row_blocks, slab, block), bf16),
            pltpu.VMEM(coulomb_core.shape, bf16),
            pltpu.VMEM(coulomb_core.shape, bf16),
            pltpu.VMEM(screen_mask.shape, jnp.int32),
            pltpu.VMEM(ao_centers.shape, f32),
            pltpu.VMEM((1, total), f32),
            pltpu.VMEM(point_coords.shape, f32),
            pltpu.VMEM(lmo_coeffs.shape, bf16),
            pltpu.VMEM((blocks * slab, block), f32),
            pltpu.VMEM((blocks * slab, blocks * slab), bf16),
            pltpu.VMEM((blocks * slab, block), f32),
            pltpu.VMEM((tile_count - 1, tile_blocks, slab, block), bf16),
            pltpu.VMEM((tile_count, tile_blocks, slab, block), bf16),
            pltpu.VMEM((batch, cols), f32),
            pltpu.VMEM((tile_count - 1, batch, strip), bf16),
            pltpu.VMEM((tile_count, batch, strip), bf16),
            pltpu.VMEM((batch, strip), bf16),
            pltpu.VMEM((grid_count, batch, strip), bf16),
            pltpu.VMEM((grid_count, batch, rows), bf16),
            pltpu.SMEM((domain_blocks.shape[0], tile_blocks), f32),
            pltpu.VMEM((nx, nc, batch, strip), f32),
            dma((2, nz)),
            dma((nz - 1, chunks)),
            dma((2, nz, side)),
            dma((nz - 1, side)),
            dma((side, nz + 1)),
            dma((side, nz - 1)),
            dma((side, chunks - 1)),
            dma((side,)),
            dma((nx,)),
            dma((grid_count,)),
            dma,
            dma((11,)),
            dma,
            dma((groups, row_blocks)),
            dma((max(1, nx - 1),)),
            dma((groups, row_blocks, max(1, nx - 1))),
            dma,
            dma,
            dma,
            dma,
            dma,
            dma,
            dma,
            dma,
        ],
        compiler_params=pltpu.CompilerParams(
            collective_id=0, has_side_effects=True, vmem_limit_bytes=VMEM_LIMIT
        ),
    )(
        *[
            pltpu.with_memory_space_constraint(operand, pltpu.HBM)
            for operand in (
                sig_blocks,
                domain_blocks,
                point_values,
                density,
                coulomb_core,
                screen_mask,
                ao_centers,
                ao_widths.reshape(1, total),
                point_coords,
                lmo_coeffs,
            )
        ]
    )


def solution(mesh):
    in_specs = (
        P("grid", "tile"),
        P("grid", None),
        P("grid", "tile"),
        P(),
        P(),
        P(),
        P(),
        P(None, "grid"),
        P("tile", None),
        P(),
    )
    out_specs = P("tile", "grid")
    return jax.shard_map(shards, mesh=mesh, in_specs=in_specs, out_specs=out_specs, check_vma=False)
```
